256 devices in a mesh: mem: 64 (over x, z_lo, y, core), head: 4 (over z_hi).
Axes of the slice: x: 4, y: 4, z: 8 (z_hi: 4, z_lo: 2; z = z_hi * 2 + z_lo), core: 2. Of those that a mesh axis runs over, the one named last changes fastest.
Arguments:
- queries: bfloat16 [8192, 4096], P('mem', 'head'), may hold values from -200 to 200
- mem_keys: bfloat16 [6144, 4096], P('mem', 'head'), may hold values from -6 to 6
- mem_values: bfloat16 [6144, 4096], P('mem', 'head'), may hold values from -24 to 24
- own_values: bfloat16 [8192, 4096], P('mem', 'head'), may hold values from -6 to 6
- gate_bias: float32 [32], P('head'), may hold values from -2 to 2
- w_out: bfloat16 [4096, 4096], P('head'), may hold values from -0.09375 to 0.09375
- probes: int32 [8192, 8], P('mem'), may hold values from 0 to 383, as said below
- pattern: int32 [64, 64], replicated, may hold values from 0 to 1, as said below
Outputs:
- projected: bfloat16 [8192, 4096], P(('mem', 'head'))
The draws below stay inside these ranges and needn't reach their ends.
Inputs may be any that keep to these rules, and one draw needn't show every extreme that they name: `pattern`: entries are 0 or 1; every row has at least one 1. `probes`: the 8 clusters of a query are distinct. The first lies in a cluster block b with pattern[r, b] = 1, r being the query's block of 128 rows.
All inputs are finite; a program needn't handle non-finite values.
Results may differ from the reference program's by a relative error of at most 0.012.
Values may be sent and summed in bfloat16 or wider, within the bound.
No kernel may reach another device: no remote copies, remote signals or barrier semaphores. Data moves between devices by JAX's collectives and lax.ppermute only.
A program may use at most 128 MiB of HBM per device.

```python
import math
import jax
import jax.numpy as jnp
from jax import lax

HEADS = 32
HD = 128
D = 4096
QDEV = 128
CSIZE = 16
PROBES = 8
BLOCKS = 64
CL_DEV = 6
CLUSTERS = 384
Q = 8192
MEM = 6144


def make_all(key):
    keys_list = [jax.random.fold_in(key, 101 + number) for number in range(8)]
    level = 2 ** jax.random.randint(keys_list[0], (BLOCKS, 1), 0, 4)
    pattern = (jax.random.randint(keys_list[1], (BLOCKS, BLOCKS), 0, 8) < level).astype(jnp.int32)
    forced = jax.random.randint(keys_list[2], (BLOCKS, 1), 0, BLOCKS)
    block_ids = jnp.arange(BLOCKS, dtype=jnp.int32)
    pattern = jnp.maximum(pattern, (block_ids[None, :] == forced).astype(jnp.int32))
    anchor = jnp.arange(Q, dtype=jnp.int32) // QDEV
    row_allowed = pattern[anchor]
    block_score = row_allowed * 2 ** 24 + jax.random.randint(keys_list[3], (Q, BLOCKS), 0, 2 ** 14) * BLOCKS + block_ids[None, :]
    unused, first_block = lax.top_k(block_score, 1)
    first = first_block[:, 0] * CL_DEV + jax.random.randint(keys_list[4], (Q,), 0, CL_DEV)
    cluster_ids = jnp.arange(CLUSTERS, dtype=jnp.int32)
    cluster_score = jax.random.randint(keys_list[5], (Q, CLUSTERS), 0, 2 ** 14) * CLUSTERS + cluster_ids[None, :]
    cluster_score = jnp.where(cluster_ids[None, :] == first[:, None], -1, cluster_score)
    unused_too, others = lax.top_k(cluster_score, PROBES - 1)
    probes = jnp.concatenate([first[:, None], others], axis=1).astype(jnp.int32)
    mem_keys = jnp.clip(jax.random.normal(keys_list[6], (MEM, D), jnp.float32), -6.0, 6.0)
    queries = jnp.clip(jax.random.normal(keys_list[7], (Q, D), jnp.float32), -6.0, 6.0)
    return (pattern, probes, queries, mem_keys)


def draw_pattern(key, part):
    return make_all(key)[0]


def draw_probes(key, part):
    return make_all(key)[1]


def draw_queries(key, part):
    return make_all(key)[2].astype(jnp.bfloat16)


def draw_mem_keys(key, part):
    return make_all(key)[3].astype(jnp.bfloat16)


def block_scale(stream_key, dims, cuts, low, largest):
    def one(dim, parts):
        draws = jax.random.uniform(jax.random.fold_in(jax.random.fold_in(stream_key, 6), dim), (parts,), jnp.float32, low / len(cuts), largest / len(cuts))
        return jnp.repeat(jnp.exp(draws), dims[dim] // parts).reshape((-1,) + (1,) * (len(dims) - dim - 1))

    gain = one(*cuts[0])
    for cut in cuts[1:]:
        gain = gain * one(*cut)
    return gain


def noise(key, extent, scale, most, split=(), kind=jnp.bfloat16):
    loudness = block_scale(key, extent, split, -0.22, 0.18) if split else 1.0
    entries = jax.random.normal(key, extent, jnp.float32) * scale * loudness
    return jnp.minimum(jnp.maximum(entries, -most), most).astype(kind)


def setup_inputs(seed: int = 0) -> dict:
    key_list = jax.random.split(jax.random.key(seed), 9)
    return {
        "queries": draw_queries(jax.random.fold_in(key_list[8], 71), 0),
        "mem_keys": draw_mem_keys(jax.random.fold_in(key_list[8], 71), 0),
        "mem_values": noise(key_list[2], (MEM, D), 4.0, 24.0, ((0, 64), (1, 4))),
        "own_values": noise(key_list[3], (Q, D), 1.0, 6.0, ((0, 64), (1, 4))),
        "gate_bias": jnp.clip(jax.random.uniform(key_list[4], (HEADS,), jnp.float32, -2.0, 2.0) * block_scale(key_list[4], (HEADS,), ((0, 4),), -0.4, 0.0), -2.0, 2.0),
        "w_out": noise(key_list[5], (D, D), D ** -0.5, 0.09375, ((0, 4),)),
        "probes": draw_probes(jax.random.fold_in(key_list[8], 71), 0),
        "pattern": draw_pattern(jax.random.fold_in(key_list[8], 71), 0),
    }


def reference(queries, mem_keys, mem_values, own_values, gate_bias, w_out, probes, pattern):
    cluster_ids = jnp.arange(CLUSTERS, dtype=jnp.int32)
    probed = jnp.any(probes[:, :, None] == cluster_ids[None, None, :], axis=1)
    allowed = jnp.repeat(pattern, CL_DEV, axis=1) > 0
    keys_all = mem_keys.astype(jnp.float32).reshape(MEM, HEADS, HD)
    vals_all = mem_values.astype(jnp.float32).reshape(MEM, HEADS, HD)
    gate = jax.nn.sigmoid(gate_bias.astype(jnp.float32))[None, :, None]
    score_scale = 1.0 / math.sqrt(HD)

    def one_block(block):
        first_row = (block * QDEV).astype(jnp.int32)
        query_block = lax.dynamic_slice_in_dim(queries, first_row, QDEV, 0).astype(jnp.float32).reshape(QDEV, HEADS, HD)
        probe_block = lax.dynamic_slice_in_dim(probed, first_row, QDEV, 0)
        allowed_row = lax.dynamic_index_in_dim(allowed, block, 0, keepdims=False)
        cluster_mask = probe_block & allowed_row[None, :]
        entry_mask = jnp.repeat(cluster_mask, CSIZE, axis=1).T
        scores = jnp.einsum('khd,qhd->hkq', keys_all, query_block) * score_scale
        scores = jnp.where(entry_mask[None], scores, -jnp.inf)
        row_peak = lax.optimization_barrier(jnp.max(scores, axis=1))
        weights = jnp.where(entry_mask[None], jnp.exp(scores - row_peak[:, None, :]), 0.0)
        denominator = lax.optimization_barrier(jnp.sum(weights, axis=1))
        rounded = lax.optimization_barrier(weights.astype(jnp.bfloat16)).astype(jnp.float32)
        recalled = jnp.einsum('hkq,khd->qhd', rounded, vals_all) / denominator.T[:, :, None]
        own_part = lax.dynamic_slice_in_dim(own_values, first_row, QDEV, 0).astype(jnp.float32).reshape(QDEV, HEADS, HD)
        blended = (gate * recalled + (1.0 - gate) * own_part).reshape(QDEV, HEADS * HD).astype(jnp.bfloat16)
        return jnp.dot(blended, w_out, preferred_element_type=jnp.float32).astype(jnp.bfloat16)
    outputs = lax.map(one_block, jnp.arange(BLOCKS, dtype=jnp.int32))
    return outputs.reshape(BLOCKS * QDEV, HEADS * HD)
```

```python
import math

import jax
import jax.numpy as jnp
import numpy as np
from jax import lax
from jax.experimental import pallas as pl
from jax.experimental.pallas import tpu as pltpu
from jax.sharding import Mesh
from jax.sharding import PartitionSpec as P

HD = 128
CSIZE = 16
NEG = -1e30
EXP2_SCALE = math.log2(math.e) / math.sqrt(HD)


B_AXES = ("zl", "y")
NX, NB, NC = 4, 8, 2
ROWS_Q, ROWS_M, ROWS_P = 128, 96, 16
NQ = NB * ROWS_Q
HALF = NB * ROWS_M
CL_CHUNK = 2 * HALF // CSIZE
OFFSETS = (0, 3, 1, 2)
TILE_Q = 256


def column_table():
    col = np.arange(128)
    slot = np.minimum(col // (HALF // CSIZE), 1)
    rest = col % (HALF // CSIZE)
    block = rest // (ROWS_M // CSIZE)
    table = np.zeros((8, 128), np.int32)
    table[0] = slot
    table[1] = block * NC
    table[2] = rest % (ROWS_M // CSIZE)
    table[3] = col < CL_CHUNK
    return table


def bias_body(place_ref, probe_ref, pattern_ref, table_ref, bias_ref):
    x = place_ref[0]
    core = place_ref[1]
    slot = table_ref[0:1, :]
    pattern = pattern_ref[...].astype(jnp.float32)
    row = lax.broadcasted_iota(jnp.int32, (8, 64), 0)
    own_rows = (x * NB + row) * NC + core
    pick = (lax.broadcasted_iota(jnp.int32, (8, 64), 1) == own_rows).astype(jnp.float32)
    allowed_rows = jnp.dot(pick, pattern, preferred_element_type=jnp.float32)
    ids = []
    for b in range(NB):
        coded = probe_ref[b].astype(jnp.float32)
        number = coded[0:8] * 16.0 + coded[8:16]
        ids.append(jnp.concatenate([number] * 16, axis=0).T)
    for k, offset in enumerate(OFFSETS):
        source_x = lax.rem(x + offset, NX)
        block = source_x * (NB * NC) + table_ref[1:2, :] + jnp.where(slot == 0, core, 1 - core)
        cluster = (block * (ROWS_M // CSIZE) + table_ref[2:3, :]).astype(jnp.float32)
        spread = (lax.broadcasted_iota(jnp.int32, (64, 128), 0) == block) & (table_ref[3:4, :] > 0)
        allowed = jnp.dot(allowed_rows, spread.astype(jnp.float32), preferred_element_type=jnp.float32)
        for b in range(NB):
            hit = ids[b][:, 0:1] == cluster
            for j in range(1, 8):
                hit = hit | (ids[b][:, j : j + 1] == cluster)
            live = hit & (allowed[b : b + 1, :] > 0.5)
            bias_ref[k, b * ROWS_Q : (b + 1) * ROWS_Q, :] = jnp.where(live, 0.0, NEG).astype(jnp.bfloat16)


def make_bias(place, received, pattern, table):
    return pl.pallas_call(
        bias_body,
        grid=(1,),
        in_specs=[
            pl.BlockSpec(memory_space=pltpu.SMEM),
            pl.BlockSpec((NB, ROWS_P, 128), lambda i: (0, (ROWS_Q + 2 * ROWS_M) // ROWS_P, 0)),
            pl.BlockSpec((64, 64), lambda i: (0, 0)),
            pl.BlockSpec((8, 128), lambda i: (0, 0)),
        ],
        out_specs=pl.BlockSpec((NX, NQ, 128), lambda i: (0, 0, 0)),
        out_shape=jax.ShapeDtypeStruct((NX, NQ, 128), jnp.bfloat16),
        name="bias",
    )(place, received, pattern, table)


def chunk_body(first, last, *refs):
    q_ref, bias_ref, near_ref, far_ref = refs[:4]
    rest = refs[4:]
    if not first:
        m_in, acc_in = rest[:2]
        rest = rest[2:]
    if last:
        (out_ref,) = rest
    else:
        m_out, acc_out = rest
    entry = lax.broadcasted_iota(jnp.int32, (2 * HALF, 128), 0) // CSIZE
    onehot = (entry == lax.broadcasted_iota(jnp.int32, (2 * HALF, 128), 1)).astype(jnp.bfloat16)
    keys = jnp.concatenate([r[:, :ROWS_M, :].reshape(HALF, HD) for r in (near_ref, far_ref)], axis=0)
    values = jnp.concatenate([r[:, ROWS_M:, :].reshape(HALF, HD) for r in (near_ref, far_ref)], axis=0)
    keys = jnp.concatenate([keys, onehot], axis=1)
    values = jnp.concatenate([values, jnp.ones((2 * HALF, 128), jnp.bfloat16)], axis=1)
    per = TILE_Q // ROWS_Q
    for t in range(NQ // TILE_Q):
        span = slice(t * TILE_Q, (t + 1) * TILE_Q)
        rows = q_ref[t * per : (t + 1) * per].reshape(TILE_Q, HD)
        rows = jnp.concatenate([rows, bias_ref[0, span, :]], axis=1)
        scores = lax.dot_general(rows, keys, (((1,), (1,)), ((), ())), preferred_element_type=jnp.float32)
        peak = jnp.max(scores, axis=1, keepdims=True)
        if first:
            peak = jnp.maximum(peak, NEG / 2)
        else:
            old = m_in[span, 0:1]
            peak = jnp.maximum(peak, old)
        weights = jnp.exp2((scores - peak) * EXP2_SCALE).astype(jnp.bfloat16)
        acc = jnp.dot(weights, values, preferred_element_type=jnp.float32)
        if not first:
            acc = acc + acc_in[span, :] * jnp.exp2((old - peak) * EXP2_SCALE)
        if last:
            out = (acc[:, :HD] / acc[:, HD:]).astype(jnp.bfloat16)
            out_ref[t * per : (t + 1) * per] = out.reshape(per, ROWS_Q, HD)
        else:
            m_out[span, :] = jnp.broadcast_to(peak, (TILE_Q, 128))
            acc_out[span, :] = acc


def attend(k, received, bias, near, far, state):
    first = k == 0
    last = k == NX - 1
    kv_spec = pl.BlockSpec((NB, 2 * ROWS_M, HD), lambda i: (0, 0, 0))
    m_spec = pl.BlockSpec((NQ, 128), lambda i: (0, 0))
    acc_spec = pl.BlockSpec((NQ, 2 * HD), lambda i: (0, 0))
    in_specs = [
        pl.BlockSpec((NB, ROWS_Q, HD), lambda i: (0, 0, 0)),
        pl.BlockSpec((1, NQ, 128), lambda i: (k, 0, 0)),
        kv_spec,
        kv_spec,
    ]
    args = [received, bias, near, far]
    if not first:
        in_specs += [m_spec, acc_spec]
        args += list(state)
    if last:
        out_specs = pl.BlockSpec((NB, ROWS_Q, HD), lambda i: (0, 0, 0))
        out_shape = jax.ShapeDtypeStruct((NB, ROWS_Q, HD), jnp.bfloat16)
    else:
        out_specs = [m_spec, acc_spec]
        out_shape = [
            jax.ShapeDtypeStruct((NQ, 128), jnp.float32),
            jax.ShapeDtypeStruct((NQ, 2 * HD), jnp.float32),
        ]
    flops = 2 * NQ * 2 * HALF * 256 * 2
    return pl.pallas_call(
        lambda *refs: chunk_body(first, last, *refs),
        grid=(1,),
        in_specs=in_specs,
        out_specs=out_specs,
        out_shape=out_shape,
        cost_estimate=pl.CostEstimate(flops=flops, bytes_accessed=4 << 20, transcendentals=NQ * 2 * HALF),
        name=f"attend{k}",
    )(*args)


def project_body(gate_ref, rec_ref, own_ref, w_ref, out_ref, mixed_ref):
    @pl.when(pl.program_id(0) == 0)
    def _():
        for h in range(NB):
            gate = 1.0 / (1.0 + jnp.exp(jnp.full((1, 128), -gate_ref[h], jnp.float32)))
            span = slice(h * HD, (h + 1) * HD)
            blended = gate * rec_ref[h].astype(jnp.float32) + (1.0 - gate) * own_ref[:, span].astype(jnp.float32)
            mixed_ref[:, span] = blended.astype(jnp.bfloat16)

    out_ref[...] = jnp.dot(mixed_ref[...], w_ref[...], preferred_element_type=jnp.float32).astype(jnp.bfloat16)


def project(gate_bias, recalled, own_values, w_out):
    width = 512
    features, model = w_out.shape
    return pl.pallas_call(
        project_body,
        grid=(model // width,),
        in_specs=[
            pl.BlockSpec(memory_space=pltpu.SMEM),
            pl.BlockSpec((NB, ROWS_Q, HD), lambda i: (0, 0, 0)),
            pl.BlockSpec((ROWS_Q, features), lambda i: (0, 0)),
            pl.BlockSpec((features, width), lambda i: (0, i)),
        ],
        out_specs=pl.BlockSpec((ROWS_Q, width), lambda i: (0, i)),
        out_shape=jax.ShapeDtypeStruct((ROWS_Q, model), jnp.bfloat16),
        scratch_shapes=[pltpu.VMEM((ROWS_Q, features), jnp.bfloat16)],
        name="project",
    )(gate_bias, recalled, own_values, w_out)


def local(queries, mem_keys, mem_values, own_values, gate_bias, w_out, probes, pattern):
    coded = probes.T
    coded = jnp.concatenate([coded // 16, coded % 16], axis=0).astype(jnp.bfloat16)

    def by_head(array):
        return array.reshape(array.shape[0], NB, HD).transpose(1, 0, 2)

    payload = jnp.concatenate(
        [
            by_head(queries),
            by_head(mem_keys),
            by_head(mem_values),
            jnp.broadcast_to(coded[None], (NB, ROWS_P, 128)),
        ],
        axis=1,
    )
    received = lax.all_to_all(payload, B_AXES, 0, 0, tiled=True)
    own = received[:, ROWS_Q : ROWS_Q + 2 * ROWS_M, :]

    def shift(array, by):
        return lax.ppermute(array, "x", [(i, (i + by) % NX) for i in range(NX)])

    def swap(array):
        return lax.ppermute(array, "c", [(0, 1), (1, 0)])

    near = [own, shift(own, 1), shift(own, 3), shift(own, 2)]
    far = [swap(array) for array in near]
    place = jnp.stack([lax.axis_index("x"), lax.axis_index("c")]).astype(jnp.int32)
    bias = make_bias(place, received, pattern, jnp.asarray(column_table()))
    state = None
    for k in range(NX):
        state = attend(k, received, bias, near[k], far[k], state)
    recalled = lax.all_to_all(state, B_AXES, 0, 0, tiled=True)
    partial = project(gate_bias, recalled, own_values, w_out)
    pieces = lax.all_to_all(partial, "h", 0, 0, tiled=True)
    pieces = pieces.reshape(4, pieces.shape[0] // 4, pieces.shape[1])
    return jnp.sum(pieces.astype(jnp.float32), axis=0).astype(jnp.bfloat16)


def solution(mesh):
    fine = Mesh(mesh.devices.reshape(NX, 2, 4, NC, 4), ("x", "zl", "y", "c", "h"))
    mem = ("x", "zl", "y", "c")
    in_specs = (
        P(mem, "h"),
        P(mem, "h"),
        P(mem, "h"),
        P(mem, "h"),
        P("h"),
        P("h", None),
        P(mem, None),
        P(),
    )
    return jax.shard_map(local, mesh=fine, in_specs=in_specs, out_specs=P((*mem, "h"), None), check_vma=False)
```

```python
import math

import jax
import jax.numpy as jnp
from jax import lax
from jax.experimental import pallas as pl
from jax.experimental.pallas import tpu as pltpu
from jax.sharding import Mesh
from jax.sharding import PartitionSpec as P

HD = 128
CSIZE = 16
NEG = -1e30
EXP2_SCALE = math.log2(math.e) / math.sqrt(HD)


B_AXES = ("zl", "y")
NX, NB, NC = 4, 8, 2
ROWS_Q, ROWS_M, ROWS_P = 128, 96, 32
NQ = NB * ROWS_Q
HALF = NB * ROWS_M
OFFSETS = (0, 3, 1, 2)
TILE_Q = 256


def in_vmem(array):
    return pltpu.with_memory_space_constraint(array, pltpu.VMEM)


VMEM_SPEC = pl.BlockSpec(memory_space=pltpu.VMEM)
SMEM_SPEC = pl.BlockSpec(memory_space=pltpu.SMEM)


def bias_body(place_ref, probe_ref, pattern_ref, bias_ref):
    x = place_ref[0]
    core = place_ref[1]
    pattern = pattern_ref[...].astype(jnp.float32)
    row = lax.broadcasted_iota(jnp.int32, (8, 64), 0)
    own_rows = (x * NB + row) * NC + core
    pick = (lax.broadcasted_iota(jnp.int32, (8, 64), 1) == own_rows).astype(jnp.float32)
    allowed_rows = jnp.dot(pick, pattern, preferred_element_type=jnp.float32)
    per_block = ROWS_M // CSIZE
    per_slot = HALF // CSIZE
    block = lax.broadcasted_iota(jnp.int32, (64, 128), 0)
    col = lax.broadcasted_iota(jnp.int32, (64, 128), 1)
    slot = jnp.where((block % NC) == core, 0, 1)
    first_col = slot * per_slot + ((block // NC) % NB) * per_block
    inside = (col >= first_col) & (col < first_col + per_block)
    allowed = []
    for offset in OFFSETS:
        spread = inside & ((block // (NC * NB)) == lax.rem(x + offset, NX))
        spread = jnp.where(spread, 1.0, 0.0)
        picked = jnp.dot(allowed_rows, spread, preferred_element_type=jnp.float32)
        allowed.append(jnp.where(picked > 0.5, 0.0, NEG))
    lane = lax.broadcasted_iota(jnp.int32, (1, 128), 1)
    targets = []
    for offset in OFFSETS:
        targets.append((lane + lax.rem(x + offset, NX) * 128).astype(jnp.float32))
    for b in range(NB):
        coded = probe_ref[b].astype(jnp.float32)
        code = coded[0:8] * 128.0 + coded[8:16]
        code = code + jnp.where(coded[16:24] == core.astype(jnp.float32), 0.0, float(per_slot))
        code = jnp.concatenate([code] * 16, axis=0).T
        for row in range(0, ROWS_Q, 32):
            live = [jnp.full((32, 128), NEG, jnp.float32)] * NX
            for j in range(8):
                spread = jnp.broadcast_to(code[row : row + 32, j : j + 1], (32, 128))
                for k in range(NX):
                    live[k] = jnp.where(spread == targets[k], allowed[k][b : b + 1, :], live[k])
            for k in range(NX):
                span = slice(b * ROWS_Q + row, b * ROWS_Q + row + 32)
                bias_ref[k, span, :] = live[k].astype(jnp.bfloat16)


def make_bias(place, probe_rows, pattern):
    return pl.pallas_call(
        bias_body,
        in_specs=[SMEM_SPEC, VMEM_SPEC, VMEM_SPEC],
        out_specs=VMEM_SPEC,
        out_shape=pltpu.VMEM((NX, NQ, 128), jnp.bfloat16),
        compiler_params=pltpu.CompilerParams(vmem_limit_bytes=16 << 20),
        name="bias",
    )(place, in_vmem(probe_rows), in_vmem(pattern))


def chunk_body(k, parts, *refs):
    first = k == 0
    last = k == NX - 1
    received_ref, bias_ref = refs[:2]
    kv_refs = refs[2 : 2 + 2 * parts]
    rest = refs[2 + 2 * parts :]
    if not first:
        m_in, acc_in = rest[:2]
        rest = rest[2:]
    if last:
        out_ref, score_ref, peak_ref = rest
    else:
        m_out, acc_out, score_ref, peak_ref = rest
    width = 256
    entry = lax.broadcasted_iota(jnp.int32, (2 * HALF, 128), 0) // CSIZE
    onehot = (entry == lax.broadcasted_iota(jnp.int32, (2 * HALF, 128), 1)).astype(jnp.bfloat16)
    if parts == 1:
        keys = [r[:, :ROWS_M, :].reshape(HALF, HD) for r in kv_refs]
        values = [r[:, ROWS_M:, :].reshape(HALF, HD) for r in kv_refs]
    else:
        keys = [r[...].reshape(HALF, HD) for r in kv_refs[0::2]]
        values = [r[...].reshape(HALF, HD) for r in kv_refs[1::2]]
    keys = jnp.concatenate([jnp.concatenate(keys, axis=0), onehot], axis=1)
    values = jnp.concatenate([jnp.concatenate(values, axis=0), jnp.ones((2 * HALF, 128), jnp.bfloat16)], axis=1)
    rows = received_ref[:, :ROWS_Q, :].reshape(NQ, HD)
    rows = jnp.concatenate([rows, bias_ref[k]], axis=1)
    for j in range(2 * HALF // width):
        span = slice(j * width, (j + 1) * width)
        scores = lax.dot_general(rows, keys[span], (((1,), (1,)), ((), ())), preferred_element_type=jnp.float32)
        score_ref[:, span] = scores
        peak = jnp.maximum(scores[:, :128], scores[:, 128:])
        if j:
            peak = jnp.maximum(peak, peak_ref[...])
        peak_ref[...] = peak
    for t in range(NQ // TILE_Q):
        span = slice(t * TILE_Q, (t + 1) * TILE_Q)
        peak = jnp.max(peak_ref[span, :], axis=1, keepdims=True)
        if first:
            peak = jnp.maximum(peak, NEG / 2)
        else:
            old = m_in[span, 0:1]
            peak = jnp.maximum(peak, old)
        weights = jnp.exp2((score_ref[span, :] - peak) * EXP2_SCALE).astype(jnp.bfloat16)
        acc = jnp.dot(weights, values, preferred_element_type=jnp.float32)
        if not first:
            acc = acc + acc_in[span, :] * jnp.exp2((old - peak) * EXP2_SCALE)
        if last:
            out = (acc[:, :HD] / acc[:, HD:]).astype(jnp.bfloat16)
            per = TILE_Q // ROWS_Q
            out_ref[t * per : (t + 1) * per] = out.reshape(per, ROWS_Q, HD)
        else:
            m_out[span, :] = jnp.broadcast_to(peak, (TILE_Q, 128))
            acc_out[span, :] = acc


def attend(k, received, bias, kv, state):
    first = k == 0
    last = k == NX - 1
    parts = len(kv) // 2
    args = [received, bias, *kv]
    if not first:
        args += list(state)
    if last:
        out_shape = pltpu.VMEM((NB, ROWS_Q, HD), jnp.bfloat16)
    else:
        out_shape = [pltpu.VMEM((NQ, 128), jnp.float32), pltpu.VMEM((NQ, 2 * HD), jnp.float32)]
    flops = 2 * NQ * 2 * HALF * 256 * 2
    return pl.pallas_call(
        lambda *refs: chunk_body(k, parts, *refs),
        in_specs=[VMEM_SPEC] * len(args),
        out_specs=VMEM_SPEC if last else [VMEM_SPEC] * 2,
        out_shape=out_shape,
        scratch_shapes=[pltpu.VMEM((NQ, 2 * HALF), jnp.float32), pltpu.VMEM((NQ, 128), jnp.float32)],
        cost_estimate=pl.CostEstimate(flops=flops, bytes_accessed=4 << 20, transcendentals=NQ * 2 * HALF),
        compiler_params=pltpu.CompilerParams(vmem_limit_bytes=24 << 20),
        name=f"attend{k}",
    )(*[in_vmem(arg) for arg in args])


def project_body(gate_ref, rec_ref, own_ref, w_ref, out_ref):
    mixed = []
    for h in range(NB):
        gate = 1.0 / (1.0 + jnp.exp(jnp.full((1, 128), -gate_ref[h], jnp.float32)))
        span = slice(h * HD, (h + 1) * HD)
        blended = gate * rec_ref[h].astype(jnp.float32) + (1.0 - gate) * own_ref[:, span].astype(jnp.float32)
        mixed.append(blended.astype(jnp.bfloat16))
    mixed = jnp.concatenate(mixed, axis=1)
    width = 512
    for i in range(w_ref.shape[1] // width):
        span = slice(i * width, (i + 1) * width)
        out_ref[:, span] = jnp.dot(mixed, w_ref[:, span], preferred_element_type=jnp.float32).astype(jnp.bfloat16)


def project(gate_bias, recalled, own_values, w_out):
    return pl.pallas_call(
        project_body,
        in_specs=[SMEM_SPEC, VMEM_SPEC, VMEM_SPEC, VMEM_SPEC],
        out_specs=VMEM_SPEC,
        out_shape=pltpu.VMEM((ROWS_Q, w_out.shape[1]), jnp.bfloat16),
        cost_estimate=pl.CostEstimate(flops=2 * ROWS_Q * w_out.size, bytes_accessed=10 << 20, transcendentals=0),
        compiler_params=pltpu.CompilerParams(vmem_limit_bytes=16 << 20),
        name="project",
    )(gate_bias, in_vmem(recalled), in_vmem(own_values), in_vmem(w_out))


def pack_body(q_ref, k_ref, v_ref, probe_ref, out_ref, sems):
    copies = []
    for h in range(NB):
        span = slice(h * HD, (h + 1) * HD)
        row = 0
        for source in (q_ref, k_ref, v_ref):
            size = source.shape[0]
            place = out_ref.at[h, row : row + size, :]
            copies.append(pltpu.make_async_copy(source.at[:, span], place, sems.at[len(copies)]))
            row += size
    for copy in copies:
        copy.start()
    per_block = ROWS_M // CSIZE
    number = probe_ref[...].astype(jnp.float32)
    block = jnp.floor((number + 0.5) * (1.0 / per_block))
    rest = number - per_block * block
    pair = jnp.floor(block * (1.0 / NC))
    source_x = jnp.floor(block * (1.0 / (NC * NB)))
    column = (pair - NB * source_x) * per_block + rest
    coded = jnp.concatenate([source_x, column, block - NC * pair, jnp.zeros_like(block)], axis=0)
    coded = coded.astype(jnp.bfloat16)
    for h in range(NB):
        out_ref[h, ROWS_Q + 2 * ROWS_M :, :] = coded
    for copy in copies:
        copy.wait()


def pack(queries, mem_keys, mem_values, probe_rows):
    anywhere = pl.BlockSpec(memory_space=pltpu.HBM)
    return pl.pallas_call(
        pack_body,
        in_specs=[anywhere, anywhere, anywhere, VMEM_SPEC],
        out_specs=VMEM_SPEC,
        out_shape=pltpu.VMEM((NB, ROWS_Q + 2 * ROWS_M + ROWS_P, HD), jnp.bfloat16),
        scratch_shapes=[pltpu.SemaphoreType.DMA((3 * NB,))],
        compiler_params=pltpu.CompilerParams(vmem_limit_bytes=16 << 20),
        name="pack",
    )(*[pltpu.with_memory_space_constraint(a, pltpu.HBM) for a in (queries, mem_keys, mem_values)], probe_rows)


def local(queries, mem_keys, mem_values, own_values, gate_bias, w_out, probes, pattern):
    received = lax.all_to_all(pack(queries, mem_keys, mem_values, probes.T), B_AXES, 0, 0, tiled=True)
    own = received[:, ROWS_Q : ROWS_Q + 2 * ROWS_M, :]

    def shift(array, by):
        return lax.ppermute(array, "x", [(i, (i + by) % NX) for i in range(NX)])

    def swap(array):
        return lax.ppermute(array, "c", [(0, 1), (1, 0)])

    place = jnp.stack([lax.axis_index("x"), lax.axis_index("c")]).astype(jnp.int32)
    left = shift(own, 1)
    right = shift(own, 3)
    own_far = swap(own)
    bias = make_bias(place, received[:, ROWS_Q + 2 * ROWS_M :, :], pattern)
    state = attend(0, received, bias, (own, own_far), None)
    left, right, *state = lax.optimization_barrier((left, right, *state))
    opposite = (shift(left[:, :ROWS_M], 1), shift(right[:, ROWS_M:], 3))
    left_far = swap(left)
    right_far = swap(right)
    state = attend(1, received, bias, (left, left_far), state)
    state = attend(2, received, bias, (right, right_far), state)
    opposite_k, opposite_v, *state = lax.optimization_barrier((*opposite, *state))
    opposite = (opposite_k, opposite_v, swap(opposite_k), swap(opposite_v))
    state = attend(3, received, bias, opposite, state)
    recalled = lax.all_to_all(state, B_AXES, 0, 0, tiled=True)
    partial = project(gate_bias, recalled, own_values, w_out)
    pieces = lax.all_to_all(partial, "h", 0, 0, tiled=True)
    pieces = pieces.reshape(4, pieces.shape[0] // 4, pieces.shape[1])
    return jnp.sum(pieces.astype(jnp.float32), axis=0).astype(jnp.bfloat16)


def solution(mesh):
    fine = Mesh(mesh.devices.reshape(NX, 2, 4, NC, 4), ("x", "zl", "y", "c", "h"))
    mem = ("x", "zl", "y", "c")
    in_specs = (
        P(mem, "h"),
        P(mem, "h"),
        P(mem, "h"),
        P(mem, "h"),
        P("h"),
        P("h", None),
        P(mem, None),
        P(),
    )
    return jax.shard_map(local, mesh=fine, in_specs=in_specs, out_specs=P((*mem, "h"), None), check_vma=False)
```

```python
import math

import jax
import jax.numpy as jnp
from jax import lax
from jax.experimental import pallas as pl
from jax.experimental.pallas import tpu as pltpu
from jax.sharding import Mesh
from jax.sharding import PartitionSpec as P

HD = 128
CSIZE = 16
NEG = -1e30
EXP2_SCALE = math.log2(math.e) / math.sqrt(HD)


B_AXES = ("zl", "y")
NX, NB, NC, NH = 4, 8, 2, 4
ROWS_Q, ROWS_M, ROWS_P, ROWS_O = 128, 96, 32, 32
NQ = NB * ROWS_Q
HALF = NB * ROWS_M
OFFSETS = (0, 3, 1, 2)
TILE_Q = 256


def in_vmem(array):
    return pltpu.with_memory_space_constraint(array, pltpu.VMEM)


VMEM_SPEC = pl.BlockSpec(memory_space=pltpu.VMEM)
SMEM_SPEC = pl.BlockSpec(memory_space=pltpu.SMEM)


def bias_body(place_ref, probe_ref, pattern_ref, bias_ref):
    x = place_ref[0]
    core = place_ref[1]
    pattern = pattern_ref[...].astype(jnp.float32)
    row = lax.broadcasted_iota(jnp.int32, (8, 64), 0)
    own_rows = (x * NB + row) * NC + core
    pick = (lax.broadcasted_iota(jnp.int32, (8, 64), 1) == own_rows).astype(jnp.float32)
    allowed_rows = jnp.dot(pick, pattern, preferred_element_type=jnp.float32)
    per_block = ROWS_M // CSIZE
    per_slot = HALF // CSIZE
    block = lax.broadcasted_iota(jnp.int32, (64, 128), 0)
    col = lax.broadcasted_iota(jnp.int32, (64, 128), 1)
    slot = jnp.where((block % NC) == core, 0, 1)
    first_col = slot * per_slot + ((block // NC) % NB) * per_block
    inside = (col >= first_col) & (col < first_col + per_block)
    allowed = []
    for offset in OFFSETS:
        spread = inside & ((block // (NC * NB)) == lax.rem(x + offset, NX))
        spread = jnp.where(spread, 1.0, 0.0)
        picked = jnp.dot(allowed_rows, spread, preferred_element_type=jnp.float32)
        allowed.append(jnp.where(picked > 0.5, 0.0, NEG))
    lane = lax.broadcasted_iota(jnp.int32, (1, 128), 1)
    targets = []
    for offset in OFFSETS:
        targets.append((lane + lax.rem(x + offset, NX) * 128).astype(jnp.float32))
    for b in range(NB):
        coded = probe_ref[b].astype(jnp.float32)
        code = coded[0:8] * 128.0 + coded[8:16]
        code = code + jnp.where(coded[16:24] == core.astype(jnp.float32), 0.0, float(per_slot))
        code = jnp.concatenate([code] * 16, axis=0).T
        for row in range(0, ROWS_Q, 32):
            live = [jnp.full((32, 128), NEG, jnp.float32)] * NX
            for j in range(8):
                spread = jnp.broadcast_to(code[row : row + 32, j : j + 1], (32, 128))
                for k in range(NX):
                    live[k] = jnp.where(spread == targets[k], allowed[k][b : b + 1, :], live[k])
            for k in range(NX):
                span = slice(b * ROWS_Q + row, b * ROWS_Q + row + 32)
                bias_ref[k, span, :] = live[k].astype(jnp.bfloat16)


def make_bias(place, probe_rows, pattern):
    return pl.pallas_call(
        bias_body,
        in_specs=[SMEM_SPEC, VMEM_SPEC, VMEM_SPEC],
        out_specs=VMEM_SPEC,
        out_shape=pltpu.VMEM((NX, NQ, 128), jnp.bfloat16),
        compiler_params=pltpu.CompilerParams(vmem_limit_bytes=16 << 20),
        name="bias",
    )(place, in_vmem(probe_rows), in_vmem(pattern))


def chunk_body(k, parts, *refs):
    first = k == 0
    last = k == NX - 1
    received_ref, bias_ref = refs[:2]
    kv_refs = refs[2 : 2 + 2 * parts]
    rest = refs[2 + 2 * parts :]
    if not first:
        m_in, acc_in = rest[:2]
        rest = rest[2:]
    if last:
        out_ref, score_ref, peak_ref = rest
    else:
        m_out, acc_out, score_ref, peak_ref = rest
    width = 256
    entry = lax.broadcasted_iota(jnp.int32, (2 * HALF, 128), 0) // CSIZE
    onehot = (entry == lax.broadcasted_iota(jnp.int32, (2 * HALF, 128), 1)).astype(jnp.bfloat16)
    if parts == 1:
        keys = [r[:, :ROWS_M, :].reshape(HALF, HD) for r in kv_refs]
        values = [r[:, ROWS_M:, :].reshape(HALF, HD) for r in kv_refs]
    else:
        keys = [r[...].reshape(HALF, HD) for r in kv_refs[0::2]]
        values = [r[...].reshape(HALF, HD) for r in kv_refs[1::2]]
    keys = jnp.concatenate([jnp.concatenate(keys, axis=0), onehot], axis=1)
    values = jnp.concatenate([jnp.concatenate(values, axis=0), jnp.ones((2 * HALF, 128), jnp.bfloat16)], axis=1)
    rows = received_ref[:, :ROWS_Q, :].reshape(NQ, HD)
    rows = jnp.concatenate([rows, bias_ref[k]], axis=1)
    for j in range(2 * HALF // width):
        span = slice(j * width, (j + 1) * width)
        scores = lax.dot_general(rows, keys[span], (((1,), (1,)), ((), ())), preferred_element_type=jnp.float32)
        score_ref[:, span] = scores
        peak = jnp.maximum(scores[:, :128], scores[:, 128:])
        if j:
            peak = jnp.maximum(peak, peak_ref[...])
        peak_ref[...] = peak
    for t in range(NQ // TILE_Q):
        span = slice(t * TILE_Q, (t + 1) * TILE_Q)
        peak = jnp.max(peak_ref[span, :], axis=1, keepdims=True)
        if first:
            peak = jnp.maximum(peak, NEG / 2)
        else:
            old = m_in[span, 0:1]
            peak = jnp.maximum(peak, old)
        weights = jnp.exp2((score_ref[span, :] - peak) * EXP2_SCALE).astype(jnp.bfloat16)
        acc = jnp.dot(weights, values, preferred_element_type=jnp.float32)
        if not first:
            acc = acc + acc_in[span, :] * jnp.exp2((old - peak) * EXP2_SCALE)
        if last:
            out = (acc[:, :HD] / acc[:, HD:]).astype(jnp.bfloat16)
            per = TILE_Q // ROWS_Q
            out_ref[t * per : (t + 1) * per] = out.reshape(per, ROWS_Q, HD)
        else:
            m_out[span, :] = jnp.broadcast_to(peak, (TILE_Q, 128))
            acc_out[span, :] = acc


def attend(k, received, bias, kv, state):
    first = k == 0
    last = k == NX - 1
    parts = len(kv) // 2
    args = [received, bias, *kv]
    if not first:
        args += list(state)
    if last:
        out_shape = pltpu.VMEM((NB, ROWS_Q, HD), jnp.bfloat16)
    else:
        out_shape = [pltpu.VMEM((NQ, 128), jnp.float32), pltpu.VMEM((NQ, 2 * HD), jnp.float32)]
    return pl.pallas_call(
        lambda *refs: chunk_body(k, parts, *refs),
        in_specs=[VMEM_SPEC] * len(args),
        out_specs=VMEM_SPEC if last else [VMEM_SPEC] * 2,
        out_shape=out_shape,
        scratch_shapes=[pltpu.VMEM((NQ, 2 * HALF), jnp.float32), pltpu.VMEM((NQ, 128), jnp.float32)],
        cost_estimate=pl.CostEstimate(flops=1 << 20, bytes_accessed=1 << 10, transcendentals=0),
        compiler_params=pltpu.CompilerParams(vmem_limit_bytes=24 << 20),
    )(*[in_vmem(arg) for arg in args])


def project_body(place_ref, gate_ref, rec_ref, own_ref, w_ref, top_ref, bottom_ref, up_ref, up_free_ref, down_ref, down_free_ref, here_ref):
    plane = place_ref[2]
    order = [pl.multiple_of(lax.rem(plane + away, NH) * ROWS_O, ROWS_O) for away in (2, 1, 3, 0)]
    mixed = []
    for h in range(NB):
        gate = 1.0 / (1.0 + jnp.exp(jnp.full((1, 128), -gate_ref[h], jnp.float32)))
        span = slice(h * HD, (h + 1) * HD)
        rows = []
        for start in order:
            recalled = rec_ref[h, pl.ds(start, ROWS_O), :].astype(jnp.float32)
            blended = gate * recalled + (1.0 - gate) * own_ref[pl.ds(start, ROWS_O), span].astype(jnp.float32)
            rows.append(blended.astype(jnp.bfloat16))
        mixed.append(jnp.concatenate(rows, axis=0))
    mixed = jnp.concatenate(mixed, axis=1)
    width = 512
    half = ROWS_O // 2
    outs = (top_ref, bottom_ref, up_ref, up_free_ref, down_free_ref, down_ref)
    for i in range(w_ref.shape[1] // width):
        span = slice(i * width, (i + 1) * width)
        part = jnp.dot(mixed, w_ref[:, span], preferred_element_type=jnp.float32)
        for n, out_ref in enumerate(outs):
            out_ref[:, span] = part[n * half : (n + 1) * half].astype(jnp.bfloat16)
        here_ref[:, span] = part[3 * ROWS_O :]


def project(place, gate_bias, recalled, own_values, w_out):
    half = pltpu.VMEM((ROWS_O // 2, w_out.shape[1]), jnp.bfloat16)
    return pl.pallas_call(
        project_body,
        in_specs=[SMEM_SPEC, SMEM_SPEC, VMEM_SPEC, VMEM_SPEC, VMEM_SPEC],
        out_specs=[VMEM_SPEC] * 7,
        out_shape=[half] * 6 + [pltpu.VMEM((ROWS_O, w_out.shape[1]), jnp.float32)],
        cost_estimate=pl.CostEstimate(flops=2 * ROWS_Q * w_out.size, bytes_accessed=10 << 20, transcendentals=0),
        compiler_params=pltpu.CompilerParams(vmem_limit_bytes=16 << 20),
        name="project",
    )(place, gate_bias, in_vmem(recalled), in_vmem(own_values), in_vmem(w_out))


def add_body(a_ref, b_ref, c_ref, d_ref, up_ref, down_ref):
    up_ref[...] = (a_ref[...].astype(jnp.float32) + b_ref[...].astype(jnp.float32)).astype(jnp.bfloat16)
    down_ref[...] = (c_ref[...].astype(jnp.float32) + d_ref[...].astype(jnp.float32)).astype(jnp.bfloat16)


def add_pairs(*args):
    half = pltpu.VMEM(args[0].shape, jnp.bfloat16)
    return pl.pallas_call(
        add_body,
        in_specs=[VMEM_SPEC] * 4,
        out_specs=[VMEM_SPEC] * 2,
        out_shape=[half] * 2,
        compiler_params=pltpu.CompilerParams(vmem_limit_bytes=16 << 20),
        name="add_pairs",
    )(*[in_vmem(arg) for arg in args])


def finish_body(here_ref, up_ref, up_free_ref, down_ref, down_free_ref, out_ref):
    half = ROWS_O // 2
    for span, a_ref, b_ref in ((slice(0, half), up_ref, down_free_ref), (slice(half, 2 * half), up_free_ref, down_ref)):
        total = here_ref[span, :] + a_ref[...].astype(jnp.float32) + b_ref[...].astype(jnp.float32)
        out_ref[span, :] = total.astype(jnp.bfloat16)


def finish(*args):
    return pl.pallas_call(
        finish_body,
        in_specs=[VMEM_SPEC] * 5,
        out_shape=jax.ShapeDtypeStruct(args[0].shape, jnp.bfloat16),
        compiler_params=pltpu.CompilerParams(vmem_limit_bytes=16 << 20),
        name="finish",
    )(*[in_vmem(arg) for arg in args])


def pack_body(q_ref, k_ref, v_ref, probe_ref, out_ref, sems):
    copies = []
    for h in range(NB):
        span = slice(h * HD, (h + 1) * HD)
        row = 0
        for source in (q_ref, k_ref, v_ref):
            size = source.shape[0]
            place = out_ref.at[h, row : row + size, :]
            copies.append(pltpu.make_async_copy(source.at[:, span], place, sems.at[len(copies)]))
            row += size
    for copy in copies:
        copy.start()
    per_block = ROWS_M // CSIZE
    number = probe_ref[...].astype(jnp.float32)
    block = jnp.floor((number + 0.5) * (1.0 / per_block))
    rest = number - per_block * block
    pair = jnp.floor(block * (1.0 / NC))
    source_x = jnp.floor(block * (1.0 / (NC * NB)))
    column = (pair - NB * source_x) * per_block + rest
    coded = jnp.concatenate([source_x, column, block - NC * pair, jnp.zeros_like(block)], axis=0)
    coded = coded.astype(jnp.bfloat16)
    for h in range(NB):
        out_ref[h, ROWS_Q + 2 * ROWS_M :, :] = coded
    for copy in copies:
        copy.wait()


def pack(queries, mem_keys, mem_values, probe_rows):
    anywhere = pl.BlockSpec(memory_space=pltpu.HBM)
    return pl.pallas_call(
        pack_body,
        in_specs=[anywhere, anywhere, anywhere, VMEM_SPEC],
        out_specs=VMEM_SPEC,
        out_shape=pltpu.VMEM((NB, ROWS_Q + 2 * ROWS_M + ROWS_P, HD), jnp.bfloat16),
        scratch_shapes=[pltpu.SemaphoreType.DMA((3 * NB,))],
        compiler_params=pltpu.CompilerParams(vmem_limit_bytes=16 << 20),
        name="pack",
    )(*[pltpu.with_memory_space_constraint(a, pltpu.HBM) for a in (queries, mem_keys, mem_values)], probe_rows)


def local(queries, mem_keys, mem_values, own_values, gate_bias, w_out, probes, pattern):
    received = lax.all_to_all(pack(queries, mem_keys, mem_values, probes.T), B_AXES, 0, 0, tiled=True)
    own = received[:, ROWS_Q : ROWS_Q + 2 * ROWS_M, :]

    def shift(array, by):
        return lax.ppermute(array, "x", [(i, (i + by) % NX) for i in range(NX)])

    def swap(array):
        return lax.ppermute(array, "c", [(0, 1), (1, 0)])

    place = jnp.stack([lax.axis_index("x"), lax.axis_index("c"), lax.axis_index("h")]).astype(jnp.int32)
    left = shift(own, 1)
    right = shift(own, 3)
    opposite = shift(own, 2)
    own_far = swap(own)
    bias = make_bias(place, received[:, ROWS_Q + 2 * ROWS_M :, :], pattern)
    state = attend(0, received, bias, (own, own_far), None)
    left, right, *state = lax.optimization_barrier((left, right, *state))
    left_far = swap(left)
    right_far = swap(right)
    state = attend(1, received, bias, (left, left_far), state)
    opposite, *state = lax.optimization_barrier((opposite, *state))
    state = attend(2, received, bias, (right, right_far), state)
    state = attend(3, received, bias, (opposite, swap(opposite)), state)
    recalled = lax.all_to_all(state, B_AXES, 0, 0, tiled=True)

    def plane_shift(array, by):
        return lax.ppermute(array, "h", [(i, (i + by) % NH) for i in range(NH)])

    top, bottom, up, up_free, down, down_free, here = project(place, gate_bias, recalled, own_values, w_out)
    top = plane_shift(top, 1)
    bottom = plane_shift(bottom, 3)
    up_free = plane_shift(up_free, 1)
    down_free = plane_shift(down_free, 3)
    up, down = add_pairs(up, top, down, bottom)
    up = plane_shift(up, 1)
    down = plane_shift(down, 3)
    return finish(here, up, up_free, down, down_free)


def solution(mesh):
    fine = Mesh(mesh.devices.reshape(NX, 2, 4, NC, 4), ("x", "zl", "y", "c", "h"))
    mem = ("x", "zl", "y", "c")
    in_specs = (
        P(mem, "h"),
        P(mem, "h"),
        P(mem, "h"),
        P(mem, "h"),
        P("h"),
        P("h", None),
        P(mem, None),
        P(),
    )
    return jax.shard_map(local, mesh=fine, in_specs=in_specs, out_specs=P((*mem, "h"), None), check_vma=False)
```

```python
import math

import jax
import jax.numpy as jnp
from jax import lax
from jax.experimental import pallas as pl
from jax.experimental.pallas import tpu as pltpu
from jax.sharding import Mesh
from jax.sharding import PartitionSpec as P

HD = 128
CSIZE = 16
NEG = -1e30
EXP2_SCALE = math.log2(math.e) / math.sqrt(HD)


B_AXES = ("zl", "y")
NX, NB, NC, NH = 4, 8, 2, 4
ROWS_Q, ROWS_M, ROWS_P, ROWS_O = 128, 96, 16, 32
NQ = NB * ROWS_Q
HALF = NB * ROWS_M
OFFSETS = (0, 3, 1, 2)
TILE_Q = 256


def in_vmem(array):
    return pltpu.with_memory_space_constraint(array, pltpu.VMEM)


VMEM_SPEC = pl.BlockSpec(memory_space=pltpu.VMEM)
SMEM_SPEC = pl.BlockSpec(memory_space=pltpu.SMEM)


def bias_body(place_ref, probe_ref, pattern_ref, bias_ref):
    x = place_ref[0]
    core = place_ref[1]
    pattern = pattern_ref[...].astype(jnp.float32)
    row = lax.broadcasted_iota(jnp.int32, (8, 64), 0)
    own_rows = (x * NB + row) * NC + core
    pick = (lax.broadcasted_iota(jnp.int32, (8, 64), 1) == own_rows).astype(jnp.float32)
    allowed_rows = jnp.dot(pick, pattern, preferred_element_type=jnp.float32)
    per_block = ROWS_M // CSIZE
    per_slot = HALF // CSIZE
    block = lax.broadcasted_iota(jnp.int32, (64, 128), 0)
    col = lax.broadcasted_iota(jnp.int32, (64, 128), 1)
    slot = jnp.where((block % NC) == core, 0, 1)
    first_col = slot * per_slot + ((block // NC) % NB) * per_block
    inside = (col >= first_col) & (col < first_col + per_block)
    allowed = []
    for offset in OFFSETS:
        spread = inside & ((block // (NC * NB)) == lax.rem(x + offset, NX))
        spread = jnp.where(spread, 1.0, 0.0)
        picked = jnp.dot(allowed_rows, spread, preferred_element_type=jnp.float32)
        allowed.append(jnp.where(picked > 0.5, 0.0, NEG))
    lane = lax.broadcasted_iota(jnp.int32, (1, 128), 1)
    targets = []
    for offset in OFFSETS:
        targets.append((lane + lax.rem(x + offset, NX) * 128).astype(jnp.float32))
    for b in range(NB):
        coded = probe_ref[b].astype(jnp.float32)
        source_x = jnp.floor(coded[0:8] * (1.0 / NC))
        code = source_x * 128.0 + coded[8:16]
        code = code + jnp.where(coded[0:8] - NC * source_x == core.astype(jnp.float32), 0.0, float(per_slot))
        code = jnp.concatenate([code] * 16, axis=0).T
        for row in range(0, ROWS_Q, 32):
            live = [jnp.full((32, 128), NEG, jnp.float32)] * NX
            for j in range(8):
                spread = jnp.broadcast_to(code[row : row + 32, j : j + 1], (32, 128))
                for k in range(NX):
                    live[k] = jnp.where(spread == targets[k], allowed[k][b : b + 1, :], live[k])
            for k in range(NX):
                span = slice(b * ROWS_Q + row, b * ROWS_Q + row + 32)
                bias_ref[k, span, :] = live[k].astype(jnp.bfloat16)


def make_bias(place, probe_rows, pattern):
    return pl.pallas_call(
        bias_body,
        in_specs=[SMEM_SPEC, VMEM_SPEC, VMEM_SPEC],
        out_specs=VMEM_SPEC,
        out_shape=pltpu.VMEM((NX, NQ, 128), jnp.bfloat16),
        compiler_params=pltpu.CompilerParams(vmem_limit_bytes=16 << 20),
        name="bias",
    )(place, in_vmem(probe_rows), in_vmem(pattern))


def chunk_body(k, parts, *refs):
    first = k == 0
    last = k == NX - 1
    received_ref, bias_ref = refs[:2]
    kv_refs = refs[2 : 2 + 2 * parts]
    rest = refs[2 + 2 * parts :]
    if not first:
        m_in, acc_in = rest[:2]
        rest = rest[2:]
    if last:
        out_ref, score_ref, peak_ref = rest
    else:
        m_out, acc_out, score_ref, peak_ref = rest
    width = 256
    entry = lax.broadcasted_iota(jnp.int32, (2 * HALF, 128), 0) // CSIZE
    onehot = (entry == lax.broadcasted_iota(jnp.int32, (2 * HALF, 128), 1)).astype(jnp.bfloat16)
    if parts == 1:
        keys = [r[:, :ROWS_M, :].reshape(HALF, HD) for r in kv_refs]
        values = [r[:, ROWS_M:, :].reshape(HALF, HD) for r in kv_refs]
    else:
        keys = [r[...].reshape(HALF, HD) for r in kv_refs[0::2]]
        values = [r[...].reshape(HALF, HD) for r in kv_refs[1::2]]
    keys = jnp.concatenate([jnp.concatenate(keys, axis=0), onehot], axis=1)
    values = jnp.concatenate([jnp.concatenate(values, axis=0), jnp.ones((2 * HALF, 128), jnp.bfloat16)], axis=1)
    rows = received_ref[:, :ROWS_Q, :].reshape(NQ, HD)
    rows = jnp.concatenate([rows, bias_ref[k]], axis=1)
    for j in range(2 * HALF // width):
        span = slice(j * width, (j + 1) * width)
        scores = lax.dot_general(rows, keys[span], (((1,), (1,)), ((), ())), preferred_element_type=jnp.float32)
        score_ref[:, span] = scores
        peak = jnp.maximum(scores[:, :128], scores[:, 128:])
        if j:
            peak = jnp.maximum(peak, peak_ref[...])
        peak_ref[...] = peak
    for t in range(NQ // TILE_Q):
        span = slice(t * TILE_Q, (t + 1) * TILE_Q)
        peak = jnp.max(peak_ref[span, :], axis=1, keepdims=True)
        if first:
            peak = jnp.maximum(peak, NEG / 2)
        else:
            old = m_in[span, 0:1]
            peak = jnp.maximum(peak, old)
        weights = jnp.exp2((score_ref[span, :] - peak) * EXP2_SCALE).astype(jnp.bfloat16)
        acc = jnp.dot(weights, values, preferred_element_type=jnp.float32)
        if not first:
            acc = acc + acc_in[span, :] * jnp.exp2((old - peak) * EXP2_SCALE)
        if last:
            out = (acc[:, :HD] / acc[:, HD:]).astype(jnp.bfloat16)
            per = TILE_Q // ROWS_Q
            out_ref[t * per : (t + 1) * per] = out.reshape(per, ROWS_Q, HD)
        else:
            m_out[span, :] = jnp.broadcast_to(peak, (TILE_Q, 128))
            acc_out[span, :] = acc


def attend(k, received, bias, kv, state):
    first = k == 0
    last = k == NX - 1
    parts = len(kv) // 2
    args = [received, bias, *kv]
    if not first:
        args += list(state)
    if last:
        out_shape = pltpu.VMEM((NB, ROWS_Q, HD), jnp.bfloat16)
    else:
        out_shape = [pltpu.VMEM((NQ, 128), jnp.float32), pltpu.VMEM((NQ, 2 * HD), jnp.float32)]
    return pl.pallas_call(
        lambda *refs: chunk_body(k, parts, *refs),
        in_specs=[VMEM_SPEC] * len(args),
        out_specs=VMEM_SPEC if last else [VMEM_SPEC] * 2,
        out_shape=out_shape,
        scratch_shapes=[pltpu.VMEM((NQ, 2 * HALF), jnp.float32), pltpu.VMEM((NQ, 128), jnp.float32)],
        cost_estimate=pl.CostEstimate(flops=1 << 20, bytes_accessed=1 << 10, transcendentals=0),
        compiler_params=pltpu.CompilerParams(vmem_limit_bytes=24 << 20),
    )(*[in_vmem(arg) for arg in args])


def project_body(place_ref, gate_ref, rec_ref, own_ref, w_ref, top_ref, bottom_ref, up_ref, up_free_ref, down_ref, down_free_ref, here_ref):
    plane = place_ref[2]
    order = [pl.multiple_of(lax.rem(plane + away, NH) * ROWS_O, ROWS_O) for away in (2, 1, 3, 0)]
    mixed = []
    for h in range(NB):
        gate = 1.0 / (1.0 + jnp.exp(jnp.full((1, 128), -gate_ref[h], jnp.float32)))
        span = slice(h * HD, (h + 1) * HD)
        rows = []
        for start in order:
            recalled = rec_ref[h, pl.ds(start, ROWS_O), :].astype(jnp.float32)
            blended = gate * recalled + (1.0 - gate) * own_ref[pl.ds(start, ROWS_O), span].astype(jnp.float32)
            rows.append(blended.astype(jnp.bfloat16))
        mixed.append(jnp.concatenate(rows, axis=0))
    mixed = jnp.concatenate(mixed, axis=1)
    width = 512
    half = ROWS_O // 2
    outs = (top_ref, bottom_ref, up_ref, up_free_ref, down_free_ref, down_ref)
    for i in range(w_ref.shape[1] // width):
        span = slice(i * width, (i + 1) * width)
        part = jnp.dot(mixed, w_ref[:, span], preferred_element_type=jnp.float32)
        for n, out_ref in enumerate(outs):
            out_ref[:, span] = part[n * half : (n + 1) * half].astype(jnp.bfloat16)
        here_ref[:, span] = part[3 * ROWS_O :]


def project(place, gate_bias, recalled, own_values, w_out):
    half = pltpu.VMEM((ROWS_O // 2, w_out.shape[1]), jnp.bfloat16)
    return pl.pallas_call(
        project_body,
        in_specs=[SMEM_SPEC, SMEM_SPEC, VMEM_SPEC, VMEM_SPEC, VMEM_SPEC],
        out_specs=[VMEM_SPEC] * 7,
        out_shape=[half] * 6 + [pltpu.VMEM((ROWS_O, w_out.shape[1]), jnp.float32)],
        cost_estimate=pl.CostEstimate(flops=2 * ROWS_Q * w_out.size, bytes_accessed=10 << 20, transcendentals=0),
        compiler_params=pltpu.CompilerParams(vmem_limit_bytes=16 << 20),
        name="project",
    )(place, gate_bias, in_vmem(recalled), in_vmem(own_values), in_vmem(w_out))


def add_body(a_ref, b_ref, out_ref):
    out_ref[...] = (a_ref[...].astype(jnp.float32) + b_ref[...].astype(jnp.float32)).astype(jnp.bfloat16)


def add(*args):
    return pl.pallas_call(
        add_body,
        in_specs=[VMEM_SPEC] * 2,
        out_specs=VMEM_SPEC,
        out_shape=pltpu.VMEM(args[0].shape, jnp.bfloat16),
        compiler_params=pltpu.CompilerParams(vmem_limit_bytes=16 << 20),
    )(*[in_vmem(arg) for arg in args])


def finish_body(here_ref, up_ref, up_free_ref, down_ref, down_free_ref, out_ref):
    half = ROWS_O // 2
    for span, a_ref, b_ref in ((slice(0, half), up_ref, down_free_ref), (slice(half, 2 * half), up_free_ref, down_ref)):
        total = here_ref[span, :] + a_ref[...].astype(jnp.float32) + b_ref[...].astype(jnp.float32)
        out_ref[span, :] = total.astype(jnp.bfloat16)


def finish(*args):
    return pl.pallas_call(
        finish_body,
        in_specs=[VMEM_SPEC] * 5,
        out_shape=jax.ShapeDtypeStruct(args[0].shape, jnp.bfloat16),
        compiler_params=pltpu.CompilerParams(vmem_limit_bytes=16 << 20),
        name="finish",
    )(*[in_vmem(arg) for arg in args])


def pack_body(q_ref, k_ref, v_ref, probe_hbm, out_ref, probe_ref, sems):
    probe_copy = pltpu.make_async_copy(probe_hbm, probe_ref, sems.at[3 * NB])
    probe_copy.start()
    copies = []
    for h in range(NB):
        span = slice(h * HD, (h + 1) * HD)
        row = 0
        for source in (q_ref, k_ref, v_ref):
            size = source.shape[0]
            place = out_ref.at[h, row : row + size, :]
            copies.append(pltpu.make_async_copy(source.at[:, span], place, sems.at[len(copies)]))
            row += size
    for copy in copies:
        copy.start()
    probe_copy.wait()
    per_block = ROWS_M // CSIZE
    number = probe_ref[...].astype(jnp.float32)
    block = jnp.floor((number + 0.5) * (1.0 / per_block))
    rest = number - per_block * block
    pair = jnp.floor(block * (1.0 / NC))
    source_x = jnp.floor(block * (1.0 / (NC * NB)))
    column = (pair - NB * source_x) * per_block + rest
    coded = jnp.concatenate([source_x * NC + block - NC * pair, column], axis=0)
    coded = coded.astype(jnp.bfloat16)
    for h in range(NB):
        out_ref[h, ROWS_Q + 2 * ROWS_M :, :] = coded
    for copy in copies:
        copy.wait()


def pack(queries, mem_keys, mem_values, probe_rows):
    anywhere = pl.BlockSpec(memory_space=pltpu.HBM)
    return pl.pallas_call(
        pack_body,
        in_specs=[anywhere] * 4,
        out_specs=VMEM_SPEC,
        out_shape=pltpu.VMEM((NB, ROWS_Q + 2 * ROWS_M + ROWS_P, HD), jnp.bfloat16),
        scratch_shapes=[pltpu.VMEM(probe_rows.shape, probe_rows.dtype), pltpu.SemaphoreType.DMA((3 * NB + 1,))],
        compiler_params=pltpu.CompilerParams(vmem_limit_bytes=16 << 20),
        name="pack",
    )(*[pltpu.with_memory_space_constraint(a, pltpu.HBM) for a in (queries, mem_keys, mem_values, probe_rows)])


def local(queries, mem_keys, mem_values, own_values, gate_bias, w_out, probes, pattern):
    received = lax.all_to_all(pack(queries, mem_keys, mem_values, probes.T), B_AXES, 0, 0, tiled=True)
    own = received[:, ROWS_Q : ROWS_Q + 2 * ROWS_M, :]

    def shift(array, by):
        return lax.ppermute(array, "x", [(i, (i + by) % NX) for i in range(NX)])

    def swap(array):
        return lax.ppermute(array, "c", [(0, 1), (1, 0)])

    place = jnp.stack([lax.axis_index("x"), lax.axis_index("c"), lax.axis_index("h")]).astype(jnp.int32)
    left = shift(own, 1)
    right = shift(own, 3)
    opposite = shift(own, 2)
    own_far = swap(own)
    bias = make_bias(place, received[:, ROWS_Q + 2 * ROWS_M :, :], pattern)
    state = attend(0, received, bias, (own, own_far), None)
    left, right, *state = lax.optimization_barrier((left, right, *state))
    left_far = swap(left)
    right_far = swap(right)
    state = attend(1, received, bias, (left, left_far), state)
    opposite, *state = lax.optimization_barrier((opposite, *state))
    state = attend(2, received, bias, (right, right_far), state)
    state = attend(3, received, bias, (opposite, swap(opposite)), state)
    recalled = lax.all_to_all(state, B_AXES, 0, 0, tiled=True)

    def plane_shift(array, by):
        return lax.ppermute(array, "h", [(i, (i + by) % NH) for i in range(NH)])

    top, bottom, up, up_free, down, down_free, here = project(place, gate_bias, recalled, own_values, w_out)
    top = plane_shift(top, 1)
    bottom = plane_shift(bottom, 3)
    up_free = plane_shift(up_free, 1)
    down_free = plane_shift(down_free, 3)
    up = plane_shift(add(up, top), 1)
    down = plane_shift(add(down, bottom), 3)
    return finish(here, up, up_free, down, down_free)


def solution(mesh):
    fine = Mesh(mesh.devices.reshape(NX, 2, 4, NC, 4), ("x", "zl", "y", "c", "h"))
    mem = ("x", "zl", "y", "c")
    in_specs = (
        P(mem, "h"),
        P(mem, "h"),
        P(mem, "h"),
        P(mem, "h"),
        P("h"),
        P("h", None),
        P(mem, None),
        P(),
    )

    return jax.shard_map(local, mesh=fine, in_specs=in_specs, out_specs=P((*mem, "h"), None), check_vma=False)
```

```python
import math

import jax
import jax.numpy as jnp
from jax import lax
from jax.experimental import pallas as pl
from jax.experimental.pallas import tpu as pltpu
from jax.sharding import Mesh
from jax.sharding import PartitionSpec as P

HD = 128
CSIZE = 16
NEG = -1e30
EXP2_SCALE = math.log2(math.e) / math.sqrt(HD)


B_AXES = ("zl", "y")
NX, NB, NC, NH = 4, 8, 2, 4
ROWS_Q, ROWS_M, ROWS_P, ROWS_O = 128, 96, 16, 32
NQ = NB * ROWS_Q
HALF = NB * ROWS_M
OFFSETS = (0, 3, 1, 2)
TILE_Q = 256


def in_vmem(array):
    return pltpu.with_memory_space_constraint(array, pltpu.VMEM)


VMEM_SPEC = pl.BlockSpec(memory_space=pltpu.VMEM)
SMEM_SPEC = pl.BlockSpec(memory_space=pltpu.SMEM)


def bias_body(place_ref, probe_ref, pattern_ref, bias_ref):
    x = place_ref[0]
    core = place_ref[1]
    pattern = pattern_ref[...].astype(jnp.float32)
    row = lax.broadcasted_iota(jnp.int32, (8, 64), 0)
    own_rows = (x * NB + row) * NC + core
    pick = (lax.broadcasted_iota(jnp.int32, (8, 64), 1) == own_rows).astype(jnp.float32)
    allowed_rows = jnp.dot(pick, pattern, preferred_element_type=jnp.float32)
    per_block = ROWS_M // CSIZE
    per_slot = HALF // CSIZE
    block = lax.broadcasted_iota(jnp.int32, (64, 128), 0)
    col = lax.broadcasted_iota(jnp.int32, (64, 128), 1)
    slot = jnp.where((block % NC) == core, 0, 1)
    first_col = slot * per_slot + ((block // NC) % NB) * per_block
    inside = (col >= first_col) & (col < first_col + per_block)
    allowed = []
    for offset in OFFSETS:
        spread = inside & ((block // (NC * NB)) == lax.rem(x + offset, NX))
        spread = jnp.where(spread, 1.0, 0.0)
        picked = jnp.dot(allowed_rows, spread, preferred_element_type=jnp.float32)
        allowed.append(jnp.where(picked > 0.5, 0.0, NEG))
    lane = lax.broadcasted_iota(jnp.int32, (1, 128), 1)
    targets = []
    for offset in OFFSETS:
        targets.append((lane + lax.rem(x + offset, NX) * 128).astype(jnp.float32))
    for b in range(NB):
        coded = probe_ref[b].astype(jnp.float32)
        source_x = jnp.floor(coded[0:8] * (1.0 / NC))
        code = source_x * 128.0 + coded[8:16]
        code = code + jnp.where(coded[0:8] - NC * source_x == core.astype(jnp.float32), 0.0, float(per_slot))
        code = jnp.concatenate([code] * 16, axis=0).T
        for row in range(0, ROWS_Q, 32):
            live = [jnp.full((32, 128), NEG, jnp.float32)] * NX
            for j in range(8):
                spread = jnp.broadcast_to(code[row : row + 32, j : j + 1], (32, 128))
                for k in range(NX):
                    live[k] = jnp.where(spread == targets[k], allowed[k][b : b + 1, :], live[k])
            for k in range(NX):
                span = slice(b * ROWS_Q + row, b * ROWS_Q + row + 32)
                bias_ref[k, span, :] = live[k].astype(jnp.bfloat16)


def make_bias(place, probe_rows, pattern):
    return pl.pallas_call(
        bias_body,
        in_specs=[SMEM_SPEC, VMEM_SPEC, VMEM_SPEC],
        out_specs=VMEM_SPEC,
        out_shape=pltpu.VMEM((NX, NQ, 128), jnp.bfloat16),
        compiler_params=pltpu.CompilerParams(vmem_limit_bytes=16 << 20),
        name="bias",
    )(place, in_vmem(probe_rows), in_vmem(pattern))


def chunk_body(k, slots, parts, first, last, *refs):
    received_ref, bias_ref = refs[:2]
    count = parts * len(slots)
    kv_refs = refs[2 : 2 + count]
    rest = refs[2 + count :]
    if not first:
        m_in, acc_in = rest[:2]
        rest = rest[2:]
    if last:
        out_ref, score_ref, peak_ref = rest
    else:
        m_out, acc_out, score_ref, peak_ref = rest
    width = 256
    size = HALF * len(slots)
    entry = lax.broadcasted_iota(jnp.int32, (size, 128), 0) // CSIZE + slots[0] * (HALF // CSIZE)
    onehot = (entry == lax.broadcasted_iota(jnp.int32, (size, 128), 1)).astype(jnp.bfloat16)
    if parts == 1:
        keys = [r[:, :ROWS_M, :].reshape(HALF, HD) for r in kv_refs]
        values = [r[:, ROWS_M:, :].reshape(HALF, HD) for r in kv_refs]
    else:
        keys = [r[...].reshape(HALF, HD) for r in kv_refs[0::2]]
        values = [r[...].reshape(HALF, HD) for r in kv_refs[1::2]]
    keys = jnp.concatenate([jnp.concatenate(keys, axis=0), onehot], axis=1)
    values = jnp.concatenate([jnp.concatenate(values, axis=0), jnp.ones((size, 128), jnp.bfloat16)], axis=1)
    rows = received_ref[:, :ROWS_Q, :].reshape(NQ, HD)
    rows = jnp.concatenate([rows, bias_ref[k]], axis=1)
    for j in range(size // width):
        span = slice(j * width, (j + 1) * width)
        scores = lax.dot_general(rows, keys[span], (((1,), (1,)), ((), ())), preferred_element_type=jnp.float32)
        score_ref[:, span] = scores
        peak = jnp.maximum(scores[:, :128], scores[:, 128:])
        if j:
            peak = jnp.maximum(peak, peak_ref[...])
        peak_ref[...] = peak
    for t in range(NQ // TILE_Q):
        span = slice(t * TILE_Q, (t + 1) * TILE_Q)
        peak = jnp.max(peak_ref[span, :], axis=1, keepdims=True)
        if first:
            peak = jnp.maximum(peak, NEG / 2)
        else:
            old = m_in[span, 0:1]
            peak = jnp.maximum(peak, old)
        weights = jnp.exp2((score_ref[span, :] - peak) * EXP2_SCALE).astype(jnp.bfloat16)
        acc = jnp.dot(weights, values, preferred_element_type=jnp.float32)
        if not first:
            acc = acc + acc_in[span, :] * jnp.exp2((old - peak) * EXP2_SCALE)
        if last:
            out = (acc[:, :HD] / acc[:, HD:]).astype(jnp.bfloat16)
            per = TILE_Q // ROWS_Q
            out_ref[t * per : (t + 1) * per] = out.reshape(per, ROWS_Q, HD)
        else:
            m_out[span, :] = jnp.broadcast_to(peak, (TILE_Q, 128))
            acc_out[span, :] = acc


def attend(k, received, bias, kv, state, slots=(0, 1), last=False):
    first = state is None
    parts = len(kv) // len(slots)
    args = [received, bias, *kv]
    if not first:
        args += list(state)
    if last:
        out_shape = pltpu.VMEM((NB, ROWS_Q, HD), jnp.bfloat16)
    else:
        out_shape = [pltpu.VMEM((NQ, 128), jnp.float32), pltpu.VMEM((NQ, 2 * HD), jnp.float32)]
    return pl.pallas_call(
        lambda *refs: chunk_body(k, slots, parts, first, last, *refs),
        in_specs=[VMEM_SPEC] * len(args),
        out_specs=VMEM_SPEC if last else [VMEM_SPEC] * 2,
        out_shape=out_shape,
        scratch_shapes=[pltpu.VMEM((NQ, HALF * len(slots)), jnp.float32), pltpu.VMEM((NQ, 128), jnp.float32)],
        cost_estimate=pl.CostEstimate(flops=1 << 20, bytes_accessed=1 << 10, transcendentals=0),
        compiler_params=pltpu.CompilerParams(vmem_limit_bytes=24 << 20),
    )(*[in_vmem(arg) for arg in args])


def project_body(place_ref, gate_ref, rec_ref, own_ref, w_ref, top_ref, bottom_ref, up_ref, up_free_ref, down_ref, down_free_ref, here_ref):
    plane = place_ref[2]
    order = [pl.multiple_of(lax.rem(plane + away, NH) * ROWS_O, ROWS_O) for away in (2, 1, 3, 0)]
    mixed = []
    for h in range(NB):
        gate = 1.0 / (1.0 + jnp.exp(jnp.full((1, 128), -gate_ref[h], jnp.float32)))
        span = slice(h * HD, (h + 1) * HD)
        rows = []
        for start in order:
            recalled = rec_ref[h, pl.ds(start, ROWS_O), :].astype(jnp.float32)
            blended = gate * recalled + (1.0 - gate) * own_ref[pl.ds(start, ROWS_O), span].astype(jnp.float32)
            rows.append(blended.astype(jnp.bfloat16))
        mixed.append(jnp.concatenate(rows, axis=0))
    mixed = jnp.concatenate(mixed, axis=1)
    width = 512
    half = ROWS_O // 2
    outs = (top_ref, bottom_ref, up_ref, up_free_ref, down_free_ref, down_ref)
    for i in range(w_ref.shape[1] // width):
        span = slice(i * width, (i + 1) * width)
        part = jnp.dot(mixed, w_ref[:, span], preferred_element_type=jnp.float32)
        for n, out_ref in enumerate(outs):
            out_ref[:, span] = part[n * half : (n + 1) * half].astype(jnp.bfloat16)
        here_ref[:, span] = part[3 * ROWS_O :]


def project(place, gate_bias, recalled, own_values, w_out):
    half = pltpu.VMEM((ROWS_O // 2, w_out.shape[1]), jnp.bfloat16)
    return pl.pallas_call(
        project_body,
        in_specs=[SMEM_SPEC, SMEM_SPEC, VMEM_SPEC, VMEM_SPEC, VMEM_SPEC],
        out_specs=[VMEM_SPEC] * 7,
        out_shape=[half] * 6 + [pltpu.VMEM((ROWS_O, w_out.shape[1]), jnp.float32)],
        cost_estimate=pl.CostEstimate(flops=2 * ROWS_Q * w_out.size, bytes_accessed=10 << 20, transcendentals=0),
        compiler_params=pltpu.CompilerParams(vmem_limit_bytes=16 << 20),
        name="project",
    )(place, gate_bias, in_vmem(recalled), in_vmem(own_values), in_vmem(w_out))


def add_body(a_ref, b_ref, out_ref):
    out_ref[...] = (a_ref[...].astype(jnp.float32) + b_ref[...].astype(jnp.float32)).astype(jnp.bfloat16)


def add(*args):
    return pl.pallas_call(
        add_body,
        in_specs=[VMEM_SPEC] * 2,
        out_specs=VMEM_SPEC,
        out_shape=pltpu.VMEM(args[0].shape, jnp.bfloat16),
        compiler_params=pltpu.CompilerParams(vmem_limit_bytes=16 << 20),
    )(*[in_vmem(arg) for arg in args])


def finish_body(here_ref, up_ref, up_free_ref, down_ref, down_free_ref, out_ref):
    half = ROWS_O // 2
    for span, a_ref, b_ref in ((slice(0, half), up_ref, down_free_ref), (slice(half, 2 * half), up_free_ref, down_ref)):
        total = here_ref[span, :] + a_ref[...].astype(jnp.float32) + b_ref[...].astype(jnp.float32)
        out_ref[span, :] = total.astype(jnp.bfloat16)


def finish(*args):
    return pl.pallas_call(
        finish_body,
        in_specs=[VMEM_SPEC] * 5,
        out_shape=jax.ShapeDtypeStruct(args[0].shape, jnp.bfloat16),
        compiler_params=pltpu.CompilerParams(vmem_limit_bytes=16 << 20),
        name="finish",
    )(*[in_vmem(arg) for arg in args])


def pack_body(q_ref, k_ref, v_ref, probe_hbm, out_ref, probe_ref, sems):
    probe_copy = pltpu.make_async_copy(probe_hbm, probe_ref, sems.at[3 * NB])
    probe_copy.start()
    copies = []
    for h in range(NB):
        span = slice(h * HD, (h + 1) * HD)
        row = 0
        for source in (q_ref, k_ref, v_ref):
            size = source.shape[0]
            place = out_ref.at[h, row : row + size, :]
            copies.append(pltpu.make_async_copy(source.at[:, span], place, sems.at[len(copies)]))
            row += size
    for copy in copies:
        copy.start()
    probe_copy.wait()
    per_block = ROWS_M // CSIZE
    number = probe_ref[...].astype(jnp.float32)
    block = jnp.floor((number + 0.5) * (1.0 / per_block))
    rest = number - per_block * block
    pair = jnp.floor(block * (1.0 / NC))
    source_x = jnp.floor(block * (1.0 / (NC * NB)))
    column = (pair - NB * source_x) * per_block + rest
    coded = jnp.concatenate([source_x * NC + block - NC * pair, column], axis=0)
    coded = coded.astype(jnp.bfloat16)
    for h in range(NB):
        out_ref[h, ROWS_Q + 2 * ROWS_M :, :] = coded
    for copy in copies:
        copy.wait()


def pack(queries, mem_keys, mem_values, probe_rows):
    anywhere = pl.BlockSpec(memory_space=pltpu.HBM)
    return pl.pallas_call(
        pack_body,
        in_specs=[anywhere] * 4,
        out_specs=VMEM_SPEC,
        out_shape=pltpu.VMEM((NB, ROWS_Q + 2 * ROWS_M + ROWS_P, HD), jnp.bfloat16),
        scratch_shapes=[pltpu.VMEM(probe_rows.shape, probe_rows.dtype), pltpu.SemaphoreType.DMA((3 * NB + 1,))],
        compiler_params=pltpu.CompilerParams(vmem_limit_bytes=16 << 20),
        name="pack",
    )(*[pltpu.with_memory_space_constraint(a, pltpu.HBM) for a in (queries, mem_keys, mem_values, probe_rows)])


def local(queries, mem_keys, mem_values, own_values, gate_bias, w_out, probes, pattern):
    received = lax.all_to_all(pack(queries, mem_keys, mem_values, probes.T), B_AXES, 0, 0, tiled=True)
    own = received[:, ROWS_Q : ROWS_Q + 2 * ROWS_M, :]

    def shift(array, by):
        return lax.ppermute(array, "x", [(i, (i + by) % NX) for i in range(NX)])

    def swap(array):
        return lax.ppermute(array, "c", [(0, 1), (1, 0)])

    place = jnp.stack([lax.axis_index("x"), lax.axis_index("c"), lax.axis_index("h")]).astype(jnp.int32)
    left = shift(own, 1)
    right = shift(own, 3)
    own_far = swap(own)
    bias = make_bias(place, received[:, ROWS_Q + 2 * ROWS_M :, :], pattern)
    state = attend(0, received, bias, (own, own_far), None)
    left, right, *state = lax.optimization_barrier((left, right, *state))
    opposite_k = shift(left[:, :ROWS_M], 1)
    opposite_v = shift(right[:, ROWS_M:], 3)
    left_far = swap(left)
    right_far = swap(right)
    state = attend(1, received, bias, (left, left_far), state)
    state = attend(2, received, bias, (right, right_far), state)
    opposite_k, opposite_v, *state = lax.optimization_barrier((opposite_k, opposite_v, *state))
    opposite_far = (swap(opposite_k), swap(opposite_v))
    state = attend(3, received, bias, (opposite_k, opposite_v), state, slots=(0,))
    state = attend(3, received, bias, opposite_far, state, slots=(1,), last=True)
    recalled = lax.all_to_all(state, B_AXES, 0, 0, tiled=True)

    def plane_shift(array, by):
        return lax.ppermute(array, "h", [(i, (i + by) % NH) for i in range(NH)])

    top, bottom, up, up_free, down, down_free, here = project(place, gate_bias, recalled, own_values, w_out)
    top = plane_shift(top, 1)
    bottom = plane_shift(bottom, 3)
    up_free = plane_shift(up_free, 1)
    down_free = plane_shift(down_free, 3)
    up = plane_shift(add(up, top), 1)
    down = plane_shift(add(down, bottom), 3)
    return finish(here, up, up_free, down, down_free)


def solution(mesh):
    fine = Mesh(mesh.devices.reshape(NX, 2, 4, NC, 4), ("x", "zl", "y", "c", "h"))
    mem = ("x", "zl", "y", "c")
    in_specs = (
        P(mem, "h"),
        P(mem, "h"),
        P(mem, "h"),
        P(mem, "h"),
        P("h"),
        P("h", None),
        P(mem, None),
        P(),
    )

    return jax.shard_map(local, mesh=fine, in_specs=in_specs, out_specs=P((*mem, "h"), None), check_vma=False)
```

```python
import math

import jax
import jax.numpy as jnp
from jax import lax
from jax.experimental import pallas as pl
from jax.experimental.pallas import tpu as pltpu
from jax.sharding import Mesh
from jax.sharding import PartitionSpec as P

HD = 128
CSIZE = 16
NEG = -1e30
EXP2_SCALE = math.log2(math.e) / math.sqrt(HD)


B_AXES = ("zl", "y")
NX, NB, NC, NH = 4, 8, 2, 4
ROWS_Q, ROWS_M, ROWS_P, ROWS_O = 128, 96, 16, 32
NQ = NB * ROWS_Q
HALF = NB * ROWS_M
OFFSETS = (0, 3, 1, 2)


def in_vmem(array):
    return pltpu.with_memory_space_constraint(array, pltpu.VMEM)


VMEM_SPEC = pl.BlockSpec(memory_space=pltpu.VMEM)
SMEM_SPEC = pl.BlockSpec(memory_space=pltpu.SMEM)


def bias_body(place_ref, probe_ref, pattern_ref, bias_ref):
    x = place_ref[0]
    core = place_ref[1]
    pattern = pattern_ref[...].astype(jnp.float32)
    row = lax.broadcasted_iota(jnp.int32, (8, 64), 0)
    own_rows = (x * NB + row) * NC + core
    pick = (lax.broadcasted_iota(jnp.int32, (8, 64), 1) == own_rows).astype(jnp.float32)
    allowed_rows = jnp.dot(pick, pattern, preferred_element_type=jnp.float32)
    per_block = ROWS_M // CSIZE
    per_slot = HALF // CSIZE
    block = lax.broadcasted_iota(jnp.int32, (64, 128), 0)
    col = lax.broadcasted_iota(jnp.int32, (64, 128), 1)
    slot = jnp.where((block % NC) == core, 0, 1)
    first_col = slot * per_slot + ((block // NC) % NB) * per_block
    inside = (col >= first_col) & (col < first_col + per_block)
    allowed = []
    for offset in OFFSETS:
        spread = inside & ((block // (NC * NB)) == lax.rem(x + offset, NX))
        spread = jnp.where(spread, 1.0, 0.0)
        picked = jnp.dot(allowed_rows, spread, preferred_element_type=jnp.float32)
        allowed.append(jnp.where(picked > 0.5, 0.0, NEG))
    lane = lax.broadcasted_iota(jnp.int32, (1, 128), 1)
    targets = []
    for offset in OFFSETS:
        targets.append((lane + lax.rem(x + offset, NX) * 128).astype(jnp.float32))
    for b in range(NB):
        coded = probe_ref[b].astype(jnp.float32)
        source_x = jnp.floor(coded[0:8] * (1.0 / NC))
        code = source_x * 128.0 + coded[8:16]
        code = code + jnp.where(coded[0:8] - NC * source_x == core.astype(jnp.float32), 0.0, float(per_slot))
        code = jnp.concatenate([code] * 16, axis=0).T
        for row in range(0, ROWS_Q, 32):
            live = [jnp.full((32, 128), NEG, jnp.float32)] * NX
            for j in range(8):
                spread = jnp.broadcast_to(code[row : row + 32, j : j + 1], (32, 128))
                for k in range(NX):
                    live[k] = jnp.where(spread == targets[k], allowed[k][b : b + 1, :], live[k])
            for k in range(NX):
                span = slice(b * ROWS_Q + row, b * ROWS_Q + row + 32)
                bias_ref[k, span, :] = live[k].astype(jnp.bfloat16)


def make_bias(place, probe_rows, pattern):
    return pl.pallas_call(
        bias_body,
        in_specs=[SMEM_SPEC, VMEM_SPEC, VMEM_SPEC],
        out_specs=VMEM_SPEC,
        out_shape=pltpu.VMEM((NX, NQ, 128), jnp.bfloat16),
        compiler_params=pltpu.CompilerParams(vmem_limit_bytes=16 << 20),
        name="bias",
    )(place, in_vmem(probe_rows), in_vmem(pattern))


def chunk_body(k, slots, parts, first, last, *refs):
    received_ref, bias_ref = refs[:2]
    count = parts * len(slots)
    kv_refs = refs[2 : 2 + count]
    rest = refs[2 + count :]
    if not first:
        m_in, acc_in = rest[:2]
        rest = rest[2:]
    if last:
        out_ref, score_ref, peak_ref = rest
    else:
        m_out, acc_out, score_ref, peak_ref = rest
    width = 256
    size = HALF * len(slots)
    entry = lax.broadcasted_iota(jnp.int32, (size, 128), 0) // CSIZE + slots[0] * (HALF // CSIZE)
    onehot = (entry == lax.broadcasted_iota(jnp.int32, (size, 128), 1)).astype(jnp.bfloat16)
    if parts == 1:
        keys = [r[:, :ROWS_M, :].reshape(HALF, HD) for r in kv_refs]
        values = [r[:, ROWS_M:, :].reshape(HALF, HD) for r in kv_refs]
    else:
        keys = [r[...].reshape(HALF, HD) for r in kv_refs[0::2]]
        values = [r[...].reshape(HALF, HD) for r in kv_refs[1::2]]
    keys = jnp.concatenate([jnp.concatenate(keys, axis=0), onehot], axis=1)
    values = jnp.concatenate([jnp.concatenate(values, axis=0), jnp.ones((size, 128), jnp.bfloat16)], axis=1)
    rows = received_ref[:, :ROWS_Q, :].reshape(NQ, HD)
    rows = jnp.concatenate([rows, bias_ref[k]], axis=1)
    for j in range(size // width):
        span = slice(j * width, (j + 1) * width)
        scores = lax.dot_general(rows, keys[span], (((1,), (1,)), ((), ())), preferred_element_type=jnp.float32)
        score_ref[:, span] = scores
        peak = jnp.maximum(scores[:, :128], scores[:, 128:])
        if j:
            peak = jnp.maximum(peak, peak_ref[...])
        peak_ref[...] = peak

    def wide(lanes, times):
        return jnp.concatenate([lanes] * times, axis=1)

    tile = 512 // len(slots) ** 2
    for t in range(NQ // tile):
        span = slice(t * tile, (t + 1) * tile)
        peak = jnp.broadcast_to(jnp.max(peak_ref[span, :], axis=1, keepdims=True), (tile, 128))
        if first:
            peak = jnp.maximum(peak, NEG / 2)
        else:
            old = m_in[span, :]
            peak = jnp.maximum(peak, old)
        weights = jnp.exp2((score_ref[span, :] - wide(peak, size // 128)) * EXP2_SCALE).astype(jnp.bfloat16)
        acc = jnp.dot(weights, values, preferred_element_type=jnp.float32)
        if not first:
            acc = acc + acc_in[span, :] * wide(jnp.exp2((old - peak) * EXP2_SCALE), 2)
        if last:
            out = (acc[:, :HD] / acc[:, HD:]).astype(jnp.bfloat16)
            per = tile // ROWS_Q
            out_ref[t * per : (t + 1) * per] = out.reshape(per, ROWS_Q, HD)
        else:
            m_out[span, :] = peak
            acc_out[span, :] = acc


def attend(k, received, bias, kv, state, slots=(0, 1), last=False):
    first = state is None
    parts = len(kv) // len(slots)
    args = [received, bias, *kv]
    if not first:
        args += list(state)
    if last:
        out_shape = pltpu.VMEM((NB, ROWS_Q, HD), jnp.bfloat16)
    else:
        out_shape = [pltpu.VMEM((NQ, 128), jnp.float32), pltpu.VMEM((NQ, 2 * HD), jnp.float32)]
    return pl.pallas_call(
        lambda *refs: chunk_body(k, slots, parts, first, last, *refs),
        in_specs=[VMEM_SPEC] * len(args),
        out_specs=VMEM_SPEC if last else [VMEM_SPEC] * 2,
        out_shape=out_shape,
        scratch_shapes=[pltpu.VMEM((NQ, HALF * len(slots)), jnp.float32), pltpu.VMEM((NQ, 128), jnp.float32)],
        cost_estimate=pl.CostEstimate(flops=1 << 20, bytes_accessed=1 << 10, transcendentals=0),
        compiler_params=pltpu.CompilerParams(vmem_limit_bytes=24 << 20),
    )(*[in_vmem(arg) for arg in args])


def project_body(place_ref, gate_ref, rec_ref, own_ref, w_ref, top_ref, bottom_ref, up_ref, up_free_ref, down_ref, down_free_ref, here_ref):
    plane = place_ref[2]
    order = [pl.multiple_of(lax.rem(plane + away, NH) * ROWS_O, ROWS_O) for away in (2, 1, 3, 0)]
    mixed = []
    for h in range(NB):
        gate = 1.0 / (1.0 + jnp.exp(jnp.full((1, 128), -gate_ref[h], jnp.float32)))
        span = slice(h * HD, (h + 1) * HD)
        rows = []
        for start in order:
            recalled = rec_ref[h, pl.ds(start, ROWS_O), :].astype(jnp.float32)
            blended = gate * recalled + (1.0 - gate) * own_ref[pl.ds(start, ROWS_O), span].astype(jnp.float32)
            rows.append(blended.astype(jnp.bfloat16))
        mixed.append(jnp.concatenate(rows, axis=0))
    mixed = jnp.concatenate(mixed, axis=1)
    width = 512
    half = ROWS_O // 2
    outs = (top_ref, bottom_ref, up_ref, up_free_ref, down_free_ref, down_ref)
    for i in range(w_ref.shape[1] // width):
        span = slice(i * width, (i + 1) * width)
        part = jnp.dot(mixed, w_ref[:, span], preferred_element_type=jnp.float32)
        for n, out_ref in enumerate(outs):
            out_ref[:, span] = part[n * half : (n + 1) * half].astype(jnp.bfloat16)
        here_ref[:, span] = part[3 * ROWS_O :]


def project(place, gate_bias, recalled, own_values, w_out):
    half = pltpu.VMEM((ROWS_O // 2, w_out.shape[1]), jnp.bfloat16)
    return pl.pallas_call(
        project_body,
        in_specs=[SMEM_SPEC, SMEM_SPEC, VMEM_SPEC, VMEM_SPEC, VMEM_SPEC],
        out_specs=[VMEM_SPEC] * 7,
        out_shape=[half] * 6 + [pltpu.VMEM((ROWS_O, w_out.shape[1]), jnp.float32)],
        cost_estimate=pl.CostEstimate(flops=2 * ROWS_Q * w_out.size, bytes_accessed=10 << 20, transcendentals=0),
        compiler_params=pltpu.CompilerParams(vmem_limit_bytes=16 << 20),
        name="project",
    )(place, gate_bias, in_vmem(recalled), in_vmem(own_values), in_vmem(w_out))


def add_body(a_ref, b_ref, out_ref):
    out_ref[...] = (a_ref[...].astype(jnp.float32) + b_ref[...].astype(jnp.float32)).astype(jnp.bfloat16)


def add(*args):
    return pl.pallas_call(
        add_body,
        in_specs=[VMEM_SPEC] * 2,
        out_specs=VMEM_SPEC,
        out_shape=pltpu.VMEM(args[0].shape, jnp.bfloat16),
        compiler_params=pltpu.CompilerParams(vmem_limit_bytes=16 << 20),
    )(*[in_vmem(arg) for arg in args])


def finish_body(here_ref, up_ref, up_free_ref, down_ref, down_free_ref, out_ref):
    half = ROWS_O // 2
    for span, a_ref, b_ref in ((slice(0, half), up_ref, down_free_ref), (slice(half, 2 * half), up_free_ref, down_ref)):
        total = here_ref[span, :] + a_ref[...].astype(jnp.float32) + b_ref[...].astype(jnp.float32)
        out_ref[span, :] = total.astype(jnp.bfloat16)


def finish(*args):
    return pl.pallas_call(
        finish_body,
        in_specs=[VMEM_SPEC] * 5,
        out_shape=jax.ShapeDtypeStruct(args[0].shape, jnp.bfloat16),
        compiler_params=pltpu.CompilerParams(vmem_limit_bytes=16 << 20),
        name="finish",
    )(*[in_vmem(arg) for arg in args])


def pack_body(q_ref, k_ref, v_ref, probe_hbm, out_ref, probe_ref, sems):
    probe_copy = pltpu.make_async_copy(probe_hbm, probe_ref, sems.at[3 * NB])
    probe_copy.start()
    copies = []
    for h in range(NB):
        span = slice(h * HD, (h + 1) * HD)
        row = 0
        for source in (q_ref, k_ref, v_ref):
            size = source.shape[0]
            place = out_ref.at[h, row : row + size, :]
            copies.append(pltpu.make_async_copy(source.at[:, span], place, sems.at[len(copies)]))
            row += size
    for copy in copies:
        copy.start()
    probe_copy.wait()
    per_block = ROWS_M // CSIZE
    number = probe_ref[...].astype(jnp.float32)
    block = jnp.floor((number + 0.5) * (1.0 / per_block))
    rest = number - per_block * block
    pair = jnp.floor(block * (1.0 / NC))
    source_x = jnp.floor(block * (1.0 / (NC * NB)))
    column = (pair - NB * source_x) * per_block + rest
    coded = jnp.concatenate([source_x * NC + block - NC * pair, column], axis=0)
    coded = coded.astype(jnp.bfloat16)
    for h in range(NB):
        out_ref[h, ROWS_Q + 2 * ROWS_M :, :] = coded
    for copy in copies:
        copy.wait()


def pack(queries, mem_keys, mem_values, probe_rows):
    anywhere = pl.BlockSpec(memory_space=pltpu.HBM)
    return pl.pallas_call(
        pack_body,
        in_specs=[anywhere] * 4,
        out_specs=VMEM_SPEC,
        out_shape=pltpu.VMEM((NB, ROWS_Q + 2 * ROWS_M + ROWS_P, HD), jnp.bfloat16),
        scratch_shapes=[pltpu.VMEM(probe_rows.shape, probe_rows.dtype), pltpu.SemaphoreType.DMA((3 * NB + 1,))],
        compiler_params=pltpu.CompilerParams(vmem_limit_bytes=16 << 20),
        name="pack",
    )(*[pltpu.with_memory_space_constraint(a, pltpu.HBM) for a in (queries, mem_keys, mem_values, probe_rows)])


def local(queries, mem_keys, mem_values, own_values, gate_bias, w_out, probes, pattern):
    received = lax.all_to_all(pack(queries, mem_keys, mem_values, probes.T), B_AXES, 0, 0, tiled=True)
    own = received[:, ROWS_Q : ROWS_Q + 2 * ROWS_M, :]

    def shift(array, by):
        return lax.ppermute(array, "x", [(i, (i + by) % NX) for i in range(NX)])

    def swap(array):
        return lax.ppermute(array, "c", [(0, 1), (1, 0)])

    place = jnp.stack([lax.axis_index("x"), lax.axis_index("c"), lax.axis_index("h")]).astype(jnp.int32)
    left = shift(own, 1)
    right = shift(own, 3)
    own_far = swap(own)
    bias = make_bias(place, received[:, ROWS_Q + 2 * ROWS_M :, :], pattern)
    state = attend(0, received, bias, (own, own_far), None)
    left, right, *state = lax.optimization_barrier((left, right, *state))
    opposite_k = shift(left[:, :ROWS_M], 1)
    opposite_v = shift(right[:, ROWS_M:], 3)
    left_far = swap(left)
    right_far = swap(right)
    state = attend(1, received, bias, (left, left_far), state)
    state = attend(2, received, bias, (right, right_far), state)
    opposite_k, opposite_v, *state = lax.optimization_barrier((opposite_k, opposite_v, *state))
    opposite_far = (swap(opposite_k), swap(opposite_v))
    state = attend(3, received, bias, (opposite_k, opposite_v), state, slots=(0,))
    state = attend(3, received, bias, opposite_far, state, slots=(1,), last=True)
    recalled = lax.all_to_all(state, B_AXES, 0, 0, tiled=True)

    def plane_shift(array, by):
        return lax.ppermute(array, "h", [(i, (i + by) % NH) for i in range(NH)])

    top, bottom, up, up_free, down, down_free, here = project(place, gate_bias, recalled, own_values, w_out)
    top = plane_shift(top, 1)
    bottom = plane_shift(bottom, 3)
    up_free = plane_shift(up_free, 1)
    down_free = plane_shift(down_free, 3)
    up = plane_shift(add(up, top), 1)
    down = plane_shift(add(down, bottom), 3)
    return finish(here, up, up_free, down, down_free)


def solution(mesh):
    fine = Mesh(mesh.devices.reshape(NX, 2, 4, NC, 4), ("x", "zl", "y", "c", "h"))
    mem = ("x", "zl", "y", "c")
    in_specs = (
        P(mem, "h"),
        P(mem, "h"),
        P(mem, "h"),
        P(mem, "h"),
        P("h"),
        P("h", None),
        P(mem, None),
        P(),
    )

    return jax.shard_map(local, mesh=fine, in_specs=in_specs, out_specs=P((*mem, "h"), None), check_vma=False)
```

```python
import math

import jax
import jax.numpy as jnp
from jax import lax
from jax.experimental import pallas as pl
from jax.experimental.pallas import tpu as pltpu
from jax.sharding import Mesh
from jax.sharding import PartitionSpec as P

HD = 128
CSIZE = 16
NEG = -1e30
EXP2_SCALE = math.log2(math.e) / math.sqrt(HD)


B_AXES = ("zl", "y")
NX, NB, NC, NH = 4, 8, 2, 4
ROWS_Q, ROWS_M, ROWS_P, ROWS_O = 128, 96, 16, 32
NQ = NB * ROWS_Q
HALF = NB * ROWS_M
OFFSETS = (0, 3, 1, 2)


def in_vmem(array):
    return pltpu.with_memory_space_constraint(array, pltpu.VMEM)


VMEM_SPEC = pl.BlockSpec(memory_space=pltpu.VMEM)
SMEM_SPEC = pl.BlockSpec(memory_space=pltpu.SMEM)


def bias_body(place_ref, probe_ref, pattern_ref, bias_ref):
    x = place_ref[0]
    core = place_ref[1]
    pattern = pattern_ref[...].astype(jnp.float32)
    row = lax.broadcasted_iota(jnp.int32, (8, 64), 0)
    own_rows = (x * NB + row) * NC + core
    pick = (lax.broadcasted_iota(jnp.int32, (8, 64), 1) == own_rows).astype(jnp.float32)
    allowed_rows = jnp.dot(pick, pattern, preferred_element_type=jnp.float32)
    per_block = ROWS_M // CSIZE
    per_slot = HALF // CSIZE
    block = lax.broadcasted_iota(jnp.int32, (64, 128), 0)
    col = lax.broadcasted_iota(jnp.int32, (64, 128), 1)
    slot = jnp.where((block % NC) == core, 0, 1)
    first_col = slot * per_slot + ((block // NC) % NB) * per_block
    inside = (col >= first_col) & (col < first_col + per_block)
    allowed = []
    for offset in OFFSETS:
        spread = inside & ((block // (NC * NB)) == lax.rem(x + offset, NX))
        spread = jnp.where(spread, 1.0, 0.0)
        picked = jnp.dot(allowed_rows, spread, preferred_element_type=jnp.float32)
        allowed.append(jnp.where(picked > 0.5, 0.0, NEG))
    lane = lax.broadcasted_iota(jnp.int32, (1, 128), 1)
    targets = []
    for offset in OFFSETS:
        targets.append((lane + lax.rem(x + offset, NX) * 128).astype(jnp.float32))
    for b in range(NB):
        coded = probe_ref[b].astype(jnp.float32)
        source_x = jnp.floor(coded[0:8] * (1.0 / NC))
        code = source_x * 128.0 + coded[8:16]
        code = code + jnp.where(coded[0:8] - NC * source_x == core.astype(jnp.float32), 0.0, float(per_slot))
        code = jnp.concatenate([code] * 16, axis=0).T
        for row in range(0, ROWS_Q, 32):
            live = [jnp.full((32, 128), NEG, jnp.float32)] * NX
            for j in range(8):
                spread = jnp.broadcast_to(code[row : row + 32, j : j + 1], (32, 128))
                for k in range(NX):
                    live[k] = jnp.where(spread == targets[k], allowed[k][b : b + 1, :], live[k])
            for k in range(NX):
                span = slice(b * ROWS_Q + row, b * ROWS_Q + row + 32)
                bias_ref[k, span, :] = live[k].astype(jnp.bfloat16)


def make_bias(place, probe_rows, pattern):
    return pl.pallas_call(
        bias_body,
        in_specs=[SMEM_SPEC, VMEM_SPEC, VMEM_SPEC],
        out_specs=VMEM_SPEC,
        out_shape=pltpu.VMEM((NX, NQ, 128), jnp.bfloat16),
        compiler_params=pltpu.CompilerParams(vmem_limit_bytes=16 << 20),
        name="bias",
    )(place, in_vmem(probe_rows), in_vmem(pattern))


def chunk_body(k, slots, parts, first, last, *refs):
    received_ref, bias_ref = refs[:2]
    count = parts * len(slots)
    kv_refs = refs[2 : 2 + count]
    rest = refs[2 + count :]
    if not first:
        m_in, acc_in = rest[:2]
        rest = rest[2:]
    if last:
        out_ref, score_ref, peak_ref = rest
    else:
        m_out, acc_out, score_ref, peak_ref = rest
    width = 256
    size = HALF * len(slots)
    entry = lax.broadcasted_iota(jnp.int32, (size, 128), 0) // CSIZE + slots[0] * (HALF // CSIZE)
    onehot = (entry == lax.broadcasted_iota(jnp.int32, (size, 128), 1)).astype(jnp.bfloat16)
    if parts == 1:
        keys = [r[:, :ROWS_M, :].reshape(HALF, HD) for r in kv_refs]
        values = [r[:, ROWS_M:, :].reshape(HALF, HD) for r in kv_refs]
    else:
        keys = [r[...].reshape(HALF, HD) for r in kv_refs[0::2]]
        values = [r[...].reshape(HALF, HD) for r in kv_refs[1::2]]
    keys = jnp.concatenate([jnp.concatenate(keys, axis=0), onehot], axis=1)
    values = jnp.concatenate([jnp.concatenate(values, axis=0), jnp.ones((size, 128), jnp.bfloat16)], axis=1)
    rows = received_ref[:, :ROWS_Q, :].reshape(NQ, HD)
    rows = jnp.concatenate([rows, bias_ref[k]], axis=1)
    for j in range(size // width):
        span = slice(j * width, (j + 1) * width)
        scores = lax.dot_general(rows, keys[span], (((1,), (1,)), ((), ())), preferred_element_type=jnp.float32)
        score_ref[:, span] = scores
        peak = jnp.maximum(scores[:, :128], scores[:, 128:])
        if j:
            peak = jnp.maximum(peak, peak_ref[...])
        peak_ref[...] = peak

    def wide(lanes, times):
        return jnp.concatenate([lanes] * times, axis=1)

    tile = 512 // len(slots) ** 2
    for t in range(NQ // tile):
        span = slice(t * tile, (t + 1) * tile)
        peak = jnp.broadcast_to(jnp.max(peak_ref[span, :], axis=1, keepdims=True), (tile, 128))
        if first:
            peak = jnp.maximum(peak, NEG / 2)
        else:
            old = m_in[span, :]
            peak = jnp.maximum(peak, old)
        weights = jnp.exp2((score_ref[span, :] - wide(peak, size // 128)) * EXP2_SCALE).astype(jnp.bfloat16)
        acc = jnp.dot(weights, values, preferred_element_type=jnp.float32)
        if not first:
            acc = acc + acc_in[span, :] * wide(jnp.exp2((old - peak) * EXP2_SCALE), 2)
        if last:
            out = (acc[:, :HD] / acc[:, HD:]).astype(jnp.bfloat16)
            per = tile // ROWS_Q
            out_ref[t * per : (t + 1) * per] = out.reshape(per, ROWS_Q, HD)
        else:
            m_out[span, :] = peak
            acc_out[span, :] = acc


def attend(k, received, bias, kv, state, slots=(0, 1), last=False):
    first = state is None
    parts = len(kv) // len(slots)
    args = [received, bias, *kv]
    if not first:
        args += list(state)
    if last:
        out_shape = pltpu.VMEM((NB, ROWS_Q, HD), jnp.bfloat16)
    else:
        out_shape = [pltpu.VMEM((NQ, 128), jnp.float32), pltpu.VMEM((NQ, 2 * HD), jnp.float32)]
    return pl.pallas_call(
        lambda *refs: chunk_body(k, slots, parts, first, last, *refs),
        in_specs=[VMEM_SPEC] * len(args),
        out_specs=VMEM_SPEC if last else [VMEM_SPEC] * 2,
        out_shape=out_shape,
        scratch_shapes=[pltpu.VMEM((NQ, HALF * len(slots)), jnp.float32), pltpu.VMEM((NQ, 128), jnp.float32)],
        cost_estimate=pl.CostEstimate(flops=1 << 20, bytes_accessed=1 << 10, transcendentals=0),
        compiler_params=pltpu.CompilerParams(vmem_limit_bytes=24 << 20),
    )(*[in_vmem(arg) for arg in args])


def project_body(place_ref, gate_ref, rec_ref, own_ref, w_ref, top_ref, bottom_ref, up_ref, up_free_ref, down_ref, down_free_ref, here_ref):
    plane = place_ref[2]
    order = [pl.multiple_of(lax.rem(plane + away, NH) * ROWS_O, ROWS_O) for away in (2, 1, 3, 0)]
    mixed = []
    for h in range(NB):
        gate = 1.0 / (1.0 + jnp.exp(jnp.full((1, 128), -gate_ref[h], jnp.float32)))
        span = slice(h * HD, (h + 1) * HD)
        rows = []
        for start in order:
            recalled = rec_ref[h, pl.ds(start, ROWS_O), :].astype(jnp.float32)
            blended = gate * recalled + (1.0 - gate) * own_ref[pl.ds(start, ROWS_O), span].astype(jnp.float32)
            rows.append(blended.astype(jnp.bfloat16))
        mixed.append(jnp.concatenate(rows, axis=0))
    mixed = jnp.concatenate(mixed, axis=1)
    width = 512
    half = ROWS_O // 2
    outs = (top_ref, bottom_ref, up_ref, up_free_ref, down_free_ref, down_ref)
    for i in range(w_ref.shape[1] // width):
        span = slice(i * width, (i + 1) * width)
        part = jnp.dot(mixed, w_ref[:, span], preferred_element_type=jnp.float32)
        for n, out_ref in enumerate(outs):
            out_ref[:, span] = part[n * half : (n + 1) * half].astype(jnp.bfloat16)
        here_ref[:, span] = part[3 * ROWS_O :]


def project(place, gate_bias, recalled, own_values, w_out):
    half = pltpu.VMEM((ROWS_O // 2, w_out.shape[1]), jnp.bfloat16)
    return pl.pallas_call(
        project_body,
        in_specs=[SMEM_SPEC, SMEM_SPEC, VMEM_SPEC, VMEM_SPEC, VMEM_SPEC],
        out_specs=[VMEM_SPEC] * 7,
        out_shape=[half] * 6 + [pltpu.VMEM((ROWS_O, w_out.shape[1]), jnp.float32)],
        cost_estimate=pl.CostEstimate(flops=2 * ROWS_Q * w_out.size, bytes_accessed=10 << 20, transcendentals=0),
        compiler_params=pltpu.CompilerParams(vmem_limit_bytes=16 << 20),
        name="project",
    )(place, gate_bias, in_vmem(recalled), in_vmem(own_values), in_vmem(w_out))


def add_body(a_ref, b_ref, out_ref):
    out_ref[...] = (a_ref[...].astype(jnp.float32) + b_ref[...].astype(jnp.float32)).astype(jnp.bfloat16)


def add(*args):
    return pl.pallas_call(
        add_body,
        in_specs=[VMEM_SPEC] * 2,
        out_specs=VMEM_SPEC,
        out_shape=pltpu.VMEM(args[0].shape, jnp.bfloat16),
        compiler_params=pltpu.CompilerParams(vmem_limit_bytes=16 << 20),
    )(*[in_vmem(arg) for arg in args])


def finish_body(half, here_ref, a_ref, b_ref, *rest):
    rows = a_ref.shape[0]
    total = here_ref[half * rows : (half + 1) * rows, :] + a_ref[...].astype(jnp.float32) + b_ref[...].astype(jnp.float32)
    rest[-1][...] = total.astype(jnp.bfloat16)


def finish(half, here, a, b, out=None):
    rows, model = a.shape
    block = pl.BlockSpec((rows, model), lambda i: (half, 0))
    args = [in_vmem(here), in_vmem(a), in_vmem(b)]
    in_specs = [VMEM_SPEC] * 3
    if out is not None:
        args.append(out)
        in_specs.append(pl.BlockSpec(memory_space=pl.ANY))
    return pl.pallas_call(
        lambda *refs: finish_body(half, *refs),
        grid=(1,),
        in_specs=in_specs,
        out_specs=block,
        out_shape=jax.ShapeDtypeStruct((2 * rows, model), jnp.bfloat16),
        input_output_aliases={} if out is None else {3: 0},
        compiler_params=pltpu.CompilerParams(vmem_limit_bytes=16 << 20),
    )(*args)


def pack_body(q_ref, k_ref, v_ref, probe_hbm, out_ref, probe_ref, sems):
    probe_copy = pltpu.make_async_copy(probe_hbm, probe_ref, sems.at[3 * NB])
    probe_copy.start()
    copies = []
    for h in range(NB):
        span = slice(h * HD, (h + 1) * HD)
        row = 0
        for source in (q_ref, k_ref, v_ref):
            size = source.shape[0]
            place = out_ref.at[h, row : row + size, :]
            copies.append(pltpu.make_async_copy(source.at[:, span], place, sems.at[len(copies)]))
            row += size
    for copy in copies:
        copy.start()
    probe_copy.wait()
    per_block = ROWS_M // CSIZE
    number = probe_ref[...].astype(jnp.float32)
    block = jnp.floor((number + 0.5) * (1.0 / per_block))
    rest = number - per_block * block
    pair = jnp.floor(block * (1.0 / NC))
    source_x = jnp.floor(block * (1.0 / (NC * NB)))
    column = (pair - NB * source_x) * per_block + rest
    coded = jnp.concatenate([source_x * NC + block - NC * pair, column], axis=0)
    coded = coded.astype(jnp.bfloat16)
    for h in range(NB):
        out_ref[h, ROWS_Q + 2 * ROWS_M :, :] = coded
    for copy in copies:
        copy.wait()


def pack(queries, mem_keys, mem_values, probe_rows):
    anywhere = pl.BlockSpec(memory_space=pltpu.HBM)
    return pl.pallas_call(
        pack_body,
        in_specs=[anywhere] * 4,
        out_specs=VMEM_SPEC,
        out_shape=pltpu.VMEM((NB, ROWS_Q + 2 * ROWS_M + ROWS_P, HD), jnp.bfloat16),
        scratch_shapes=[pltpu.VMEM(probe_rows.shape, probe_rows.dtype), pltpu.SemaphoreType.DMA((3 * NB + 1,))],
        compiler_params=pltpu.CompilerParams(vmem_limit_bytes=16 << 20),
        name="pack",
    )(*[pltpu.with_memory_space_constraint(a, pltpu.HBM) for a in (queries, mem_keys, mem_values, probe_rows)])


def local(queries, mem_keys, mem_values, own_values, gate_bias, w_out, probes, pattern):
    received = lax.all_to_all(pack(queries, mem_keys, mem_values, probes.T), B_AXES, 0, 0, tiled=True)
    own = received[:, ROWS_Q : ROWS_Q + 2 * ROWS_M, :]

    def shift(array, by):
        return lax.ppermute(array, "x", [(i, (i + by) % NX) for i in range(NX)])

    def swap(array):
        return lax.ppermute(array, "c", [(0, 1), (1, 0)])

    place = jnp.stack([lax.axis_index("x"), lax.axis_index("c"), lax.axis_index("h")]).astype(jnp.int32)
    left = shift(own, 1)
    right = shift(own, 3)
    own_far = swap(own)
    bias = make_bias(place, received[:, ROWS_Q + 2 * ROWS_M :, :], pattern)
    state = attend(0, received, bias, (own, own_far), None)
    left, *state = lax.optimization_barrier((left, *state))
    opposite_k = shift(left[:, :ROWS_M], 1)
    left_far = swap(left)
    right, *state = lax.optimization_barrier((right, *state))
    opposite_v = shift(right[:, ROWS_M:], 3)
    right_far = swap(right)
    state = attend(1, received, bias, (left, left_far), state)
    state = attend(2, received, bias, (right, right_far), state)
    opposite_k, opposite_v, *state = lax.optimization_barrier((opposite_k, opposite_v, *state))
    opposite_far = (swap(opposite_k), swap(opposite_v))
    state = attend(3, received, bias, (opposite_k, opposite_v), state, slots=(0,))
    state = attend(3, received, bias, opposite_far, state, slots=(1,), last=True)
    recalled = lax.all_to_all(state, B_AXES, 0, 0, tiled=True)

    def plane_shift(array, by):
        return lax.ppermute(array, "h", [(i, (i + by) % NH) for i in range(NH)])

    top, bottom, up, up_free, down, down_free, here = project(place, gate_bias, recalled, own_values, w_out)
    top = plane_shift(top, 1)
    bottom = plane_shift(bottom, 3)
    up_free = plane_shift(up_free, 1)
    down_free = plane_shift(down_free, 3)
    up = plane_shift(add(up, top), 1)
    down = plane_shift(add(down, bottom), 3)
    out = finish(1, here, up_free, down)
    return finish(0, here, up, down_free, out)


def solution(mesh):
    fine = Mesh(mesh.devices.reshape(NX, 2, 4, NC, 4), ("x", "zl", "y", "c", "h"))
    mem = ("x", "zl", "y", "c")
    in_specs = (
        P(mem, "h"),
        P(mem, "h"),
        P(mem, "h"),
        P(mem, "h"),
        P("h"),
        P("h", None),
        P(mem, None),
        P(),
    )

    return jax.shard_map(local, mesh=fine, in_specs=in_specs, out_specs=P((*mem, "h"), None), check_vma=False)
```

```python
import math

import jax
import jax.numpy as jnp
from jax import lax
from jax.experimental import pallas as pl
from jax.experimental.pallas import tpu as pltpu
from jax.sharding import Mesh
from jax.sharding import PartitionSpec as P

HD = 128
CSIZE = 16
NEG = -1e30
EXP2_SCALE = math.log2(math.e) / math.sqrt(HD)


B_AXES = ("zl", "y")
NX, NB, NC, NH = 4, 8, 2, 4
ROWS_Q, ROWS_M, ROWS_P, ROWS_O = 128, 96, 16, 32
ROWS_F = 120
COLS_D = 2048
NQ = NB * ROWS_Q
HALF = NB * ROWS_M
OFFSETS = (0, 3, 1, 2)


def in_vmem(array):
    return pltpu.with_memory_space_constraint(array, pltpu.VMEM)


VMEM_SPEC = pl.BlockSpec(memory_space=pltpu.VMEM)
SMEM_SPEC = pl.BlockSpec(memory_space=pltpu.SMEM)


def bias_body(place_ref, probe_ref, pattern_ref, bias_ref):
    x = place_ref[0]
    core = place_ref[1]
    pattern = pattern_ref[...].astype(jnp.float32)
    row = lax.broadcasted_iota(jnp.int32, (8, 64), 0)
    own_rows = (x * NB + row) * NC + core
    pick = (lax.broadcasted_iota(jnp.int32, (8, 64), 1) == own_rows).astype(jnp.float32)
    allowed_rows = jnp.dot(pick, pattern, preferred_element_type=jnp.float32)
    per_block = ROWS_M // CSIZE
    per_slot = HALF // CSIZE
    block = lax.broadcasted_iota(jnp.int32, (64, 128), 0)
    col = lax.broadcasted_iota(jnp.int32, (64, 128), 1)
    slot = jnp.where((block % NC) == core, 0, 1)
    first_col = slot * per_slot + ((block // NC) % NB) * per_block
    inside = (col >= first_col) & (col < first_col + per_block)
    allowed = []
    for offset in OFFSETS:
        spread = inside & ((block // (NC * NB)) == lax.rem(x + offset, NX))
        spread = jnp.where(spread, 1.0, 0.0)
        picked = jnp.dot(allowed_rows, spread, preferred_element_type=jnp.float32)
        allowed.append(jnp.where(picked > 0.5, 0.0, NEG))
    lane = lax.broadcasted_iota(jnp.int32, (1, 128), 1)
    targets = []
    for offset in OFFSETS:
        targets.append((lane + lax.rem(x + offset, NX) * 128).astype(jnp.float32))
    for b in range(NB):
        coded = probe_ref[b].astype(jnp.float32)
        source_x = jnp.floor(coded[0:8] * (1.0 / NC))
        code = source_x * 128.0 + coded[8:16]
        code = code + jnp.where(coded[0:8] - NC * source_x == core.astype(jnp.float32), 0.0, float(per_slot))
        code = jnp.concatenate([code] * 16, axis=0).T
        for row in range(0, ROWS_Q, 32):
            live = [jnp.full((32, 128), NEG, jnp.float32)] * NX
            for j in range(8):
                spread = jnp.broadcast_to(code[row : row + 32, j : j + 1], (32, 128))
                for k in range(NX):
                    live[k] = jnp.where(spread == targets[k], allowed[k][b : b + 1, :], live[k])
            for k in range(NX):
                span = slice(b * ROWS_Q + row, b * ROWS_Q + row + 32)
                bias_ref[k, span, :] = live[k].astype(jnp.bfloat16)


def make_bias(place, probe_rows, pattern):
    return pl.pallas_call(
        bias_body,
        in_specs=[SMEM_SPEC, VMEM_SPEC, VMEM_SPEC],
        out_specs=VMEM_SPEC,
        out_shape=pltpu.VMEM((NX, NQ, 128), jnp.bfloat16),
        compiler_params=pltpu.CompilerParams(vmem_limit_bytes=16 << 20),
        name="bias",
    )(place, in_vmem(probe_rows), in_vmem(pattern))


def chunk_body(k, slots, parts, first, last, *refs):
    received_ref, bias_ref = refs[:2]
    count = parts * len(slots)
    kv_refs = refs[2 : 2 + count]
    rest = refs[2 + count :]
    if not first:
        m_in, acc_in = rest[:2]
        rest = rest[2:]
    if last:
        out_ref, score_ref, peak_ref = rest
    else:
        m_out, acc_out, score_ref, peak_ref = rest
    width = 256
    size = HALF * len(slots)
    entry = lax.broadcasted_iota(jnp.int32, (size, 128), 0) // CSIZE + slots[0] * (HALF // CSIZE)
    onehot = (entry == lax.broadcasted_iota(jnp.int32, (size, 128), 1)).astype(jnp.bfloat16)
    if parts == 1:
        keys = [r[:, :ROWS_M, :].reshape(HALF, HD) for r in kv_refs]
        values = [r[:, ROWS_M:, :].reshape(HALF, HD) for r in kv_refs]
    else:
        keys = [r[:, :ROWS_M, :].reshape(HALF, HD) for r in kv_refs[0::2]]
        values = []
        for a_ref, b_ref in zip(kv_refs[0::2], kv_refs[1::2]):
            for n in range(NB):
                values += [a_ref[n, ROWS_M:, :], b_ref[n]]
    keys = jnp.concatenate([jnp.concatenate(keys, axis=0), onehot], axis=1)
    values = jnp.concatenate([jnp.concatenate(values, axis=0), jnp.ones((size, 128), jnp.bfloat16)], axis=1)
    rows = received_ref[:, :ROWS_Q, :].reshape(NQ, HD)
    rows = jnp.concatenate([rows, bias_ref[k]], axis=1)
    for j in range(size // width):
        span = slice(j * width, (j + 1) * width)
        scores = lax.dot_general(rows, keys[span], (((1,), (1,)), ((), ())), preferred_element_type=jnp.float32)
        score_ref[:, span] = scores
        peak = jnp.maximum(scores[:, :128], scores[:, 128:])
        if j:
            peak = jnp.maximum(peak, peak_ref[...])
        peak_ref[...] = peak

    def wide(lanes, times):
        return jnp.concatenate([lanes] * times, axis=1)

    tile = 512 // len(slots) ** 2
    for t in range(NQ // tile):
        span = slice(t * tile, (t + 1) * tile)
        peak = jnp.broadcast_to(jnp.max(peak_ref[span, :], axis=1, keepdims=True), (tile, 128))
        if first:
            peak = jnp.maximum(peak, NEG / 2)
        else:
            old = m_in[span, :]
            peak = jnp.maximum(peak, old)
        weights = jnp.exp2((score_ref[span, :] - wide(peak, size // 128)) * EXP2_SCALE).astype(jnp.bfloat16)
        acc = jnp.dot(weights, values, preferred_element_type=jnp.float32)
        if not first:
            acc = acc + acc_in[span, :] * wide(jnp.exp2((old - peak) * EXP2_SCALE), 2)
        if last:
            out = (acc[:, :HD] / acc[:, HD:]).astype(jnp.bfloat16)
            per = tile // ROWS_Q
            out_ref[t * per : (t + 1) * per] = out.reshape(per, ROWS_Q, HD)
        else:
            m_out[span, :] = peak
            acc_out[span, :] = acc


def attend(k, received, bias, kv, state, slots=(0, 1), last=False):
    first = state is None
    parts = len(kv) // len(slots)
    args = [received, bias, *kv]
    if not first:
        args += list(state)
    if last:
        out_shape = pltpu.VMEM((NB, ROWS_Q, HD), jnp.bfloat16)
    else:
        out_shape = [pltpu.VMEM((NQ, 128), jnp.float32), pltpu.VMEM((NQ, 2 * HD), jnp.float32)]
    return pl.pallas_call(
        lambda *refs: chunk_body(k, slots, parts, first, last, *refs),
        in_specs=[VMEM_SPEC] * len(args),
        out_specs=VMEM_SPEC if last else [VMEM_SPEC] * 2,
        out_shape=out_shape,
        scratch_shapes=[pltpu.VMEM((NQ, HALF * len(slots)), jnp.float32), pltpu.VMEM((NQ, 128), jnp.float32)],
        cost_estimate=pl.CostEstimate(flops=1 << 20, bytes_accessed=1 << 10, transcendentals=0),
        compiler_params=pltpu.CompilerParams(vmem_limit_bytes=24 << 20),
    )(*[in_vmem(arg) for arg in args])


def project_body(place_ref, gate_ref, rec_ref, own_ref, w_ref, *outs):
    plane = place_ref[2]
    starts = [pl.multiple_of(lax.rem(plane + away, NH) * ROWS_O, ROWS_O) for away in (2, 1, 3, 0)]
    mixed = []
    for h in range(NB):
        gate = 1.0 / (1.0 + jnp.exp(jnp.full((1, 128), -gate_ref[h], jnp.float32)))
        span = slice(h * HD, (h + 1) * HD)
        rows = []
        for start in starts:
            recalled = rec_ref[h, pl.ds(start, ROWS_O), :].astype(jnp.float32)
            blended = gate * recalled + (1.0 - gate) * own_ref[pl.ds(start, ROWS_O), span].astype(jnp.float32)
            rows.append(blended.astype(jnp.bfloat16))
        mixed.append(jnp.concatenate(rows, axis=0))
    mixed = jnp.concatenate(mixed, axis=1)
    here_ref = outs[-1]
    width = 256
    for i in range(w_ref.shape[1] // width):
        first = i * width
        part = jnp.dot(mixed, w_ref[:, first : first + width], preferred_element_type=jnp.float32)
        side = int(first >= COLS_D)
        at = first - side * COLS_D
        for n in range(3):
            rows = part[n * ROWS_O : (n + 1) * ROWS_O]
            outs[2 * n + side][:, at : at + width] = rows.astype(jnp.bfloat16)
        here_ref[:, first : first + width] = part[3 * ROWS_O :]


def project(place, gate_bias, recalled, own_values, w_out):
    model = w_out.shape[1]
    sides = [pltpu.VMEM((ROWS_O, cols), jnp.bfloat16) for cols in (COLS_D, model - COLS_D)]
    outs = sides * 3 + [pltpu.VMEM((ROWS_O, model), jnp.float32)]
    return pl.pallas_call(
        project_body,
        in_specs=[SMEM_SPEC, SMEM_SPEC, VMEM_SPEC, VMEM_SPEC, VMEM_SPEC],
        out_specs=[VMEM_SPEC] * len(outs),
        out_shape=outs,
        cost_estimate=pl.CostEstimate(flops=1 << 20, bytes_accessed=1 << 10, transcendentals=0),
        compiler_params=pltpu.CompilerParams(vmem_limit_bytes=16 << 20),
        name="project",
    )(place, gate_bias, in_vmem(recalled), in_vmem(own_values), in_vmem(w_out))


def add_body(a_ref, b_ref, out_ref):
    out_ref[...] = (a_ref[...].astype(jnp.float32) + b_ref[...].astype(jnp.float32)).astype(jnp.bfloat16)


def add(*args):
    return pl.pallas_call(
        add_body,
        in_specs=[VMEM_SPEC] * 2,
        out_specs=VMEM_SPEC,
        out_shape=pltpu.VMEM(args[0].shape, jnp.bfloat16),
        compiler_params=pltpu.CompilerParams(vmem_limit_bytes=16 << 20),
    )(*[in_vmem(arg) for arg in args])


def finish_body(here_ref, up_free_ref, down_ref, up_ref, down_free_ref, out_ref):
    for span, a_ref, b_ref in (
        (slice(0, COLS_D), up_free_ref, down_ref),
        (slice(COLS_D, out_ref.shape[1]), up_ref, down_free_ref),
    ):
        total = here_ref[:, span] + a_ref[...].astype(jnp.float32) + b_ref[...].astype(jnp.float32)
        out_ref[:, span] = total.astype(jnp.bfloat16)


def finish(*args):
    return pl.pallas_call(
        finish_body,
        in_specs=[VMEM_SPEC] * 5,
        out_shape=jax.ShapeDtypeStruct(args[0].shape, jnp.bfloat16),
        compiler_params=pltpu.CompilerParams(vmem_limit_bytes=16 << 20),
        name="finish",
    )(*[in_vmem(arg) for arg in args])


def pack_body(q_ref, k_ref, v_ref, probe_hbm, out_ref, probe_ref, sems):
    probe_copy = pltpu.make_async_copy(probe_hbm, probe_ref, sems.at[3 * NB])
    probe_copy.start()
    copies = []
    for h in range(NB):
        span = slice(h * HD, (h + 1) * HD)
        row = 0
        for source in (q_ref, k_ref, v_ref):
            size = source.shape[0]
            place = out_ref.at[h, row : row + size, :]
            copies.append(pltpu.make_async_copy(source.at[:, span], place, sems.at[len(copies)]))
            row += size
    for copy in copies:
        copy.start()
    probe_copy.wait()
    per_block = ROWS_M // CSIZE
    number = probe_ref[...].astype(jnp.float32)
    block = jnp.floor((number + 0.5) * (1.0 / per_block))
    rest = number - per_block * block
    pair = jnp.floor(block * (1.0 / NC))
    source_x = jnp.floor(block * (1.0 / (NC * NB)))
    column = (pair - NB * source_x) * per_block + rest
    coded = jnp.concatenate([source_x * NC + block - NC * pair, column], axis=0)
    coded = coded.astype(jnp.bfloat16)
    for h in range(NB):
        out_ref[h, ROWS_Q + 2 * ROWS_M :, :] = coded
    for copy in copies:
        copy.wait()


def pack(queries, mem_keys, mem_values, probe_rows):
    anywhere = pl.BlockSpec(memory_space=pltpu.HBM)
    return pl.pallas_call(
        pack_body,
        in_specs=[anywhere] * 4,
        out_specs=VMEM_SPEC,
        out_shape=pltpu.VMEM((NB, ROWS_Q + 2 * ROWS_M + ROWS_P, HD), jnp.bfloat16),
        scratch_shapes=[pltpu.VMEM(probe_rows.shape, probe_rows.dtype), pltpu.SemaphoreType.DMA((3 * NB + 1,))],
        compiler_params=pltpu.CompilerParams(vmem_limit_bytes=16 << 20),
        name="pack",
    )(*[pltpu.with_memory_space_constraint(a, pltpu.HBM) for a in (queries, mem_keys, mem_values, probe_rows)])


def local(queries, mem_keys, mem_values, own_values, gate_bias, w_out, probes, pattern):
    received = lax.all_to_all(pack(queries, mem_keys, mem_values, probes.T), B_AXES, 0, 0, tiled=True)
    own = received[:, ROWS_Q : ROWS_Q + 2 * ROWS_M, :]

    def shift(array, by):
        return lax.ppermute(array, "x", [(i, (i + by) % NX) for i in range(NX)])

    def swap(array):
        return lax.ppermute(array, "c", [(0, 1), (1, 0)])

    place = jnp.stack([lax.axis_index("x"), lax.axis_index("c"), lax.axis_index("h")]).astype(jnp.int32)
    left = shift(own, 1)
    right = shift(own, 3)
    own_far = swap(own)
    bias = make_bias(place, received[:, ROWS_Q + 2 * ROWS_M :, :], pattern)
    state = attend(0, received, bias, (own, own_far), None)
    left, *state = lax.optimization_barrier((left, *state))
    opposite_k = shift(left[:, :ROWS_F], 1)
    left_far = swap(left)
    right, *state = lax.optimization_barrier((right, *state))
    opposite_v = shift(right[:, ROWS_F:], 3)
    right_far = swap(right)
    state = attend(1, received, bias, (left, left_far), state)
    state = attend(2, received, bias, (right, right_far), state)
    opposite_k, opposite_v, *state = lax.optimization_barrier((opposite_k, opposite_v, *state))
    opposite_far = (swap(opposite_k), swap(opposite_v))
    state = attend(3, received, bias, (opposite_k, opposite_v), state, slots=(0,))
    state = attend(3, received, bias, opposite_far, state, slots=(1,), last=True)
    recalled = lax.all_to_all(state, B_AXES, 0, 0, tiled=True)

    def plane_shift(array, by):
        return lax.ppermute(array, "h", [(i, (i + by) % NH) for i in range(NH)])

    operands = (place, gate_bias, recalled, own_values, w_out)
    far_down, far_up, up_free, up, down, down_free, here = project(*operands)
    far_down = plane_shift(far_down, 3)
    far_up = plane_shift(far_up, 1)
    up_free = plane_shift(up_free, 1)
    down_free = plane_shift(down_free, 3)
    up = plane_shift(add(up, far_up), 1)
    down = plane_shift(add(down, far_down), 3)
    return finish(here, up_free, down, up, down_free)


def solution(mesh):
    fine = Mesh(mesh.devices.reshape(NX, 2, 4, NC, 4), ("x", "zl", "y", "c", "h"))
    mem = ("x", "zl", "y", "c")
    in_specs = (
        P(mem, "h"),
        P(mem, "h"),
        P(mem, "h"),
        P(mem, "h"),
        P("h"),
        P("h", None),
        P(mem, None),
        P(),
    )

    return jax.shard_map(local, mesh=fine, in_specs=in_specs, out_specs=P((*mem, "h"), None), check_vma=False)
```

```python
import math

import jax
import jax.numpy as jnp
from jax import lax
from jax.experimental import pallas as pl
from jax.experimental.pallas import tpu as pltpu
from jax.sharding import Mesh
from jax.sharding import PartitionSpec as P

HD = 128
CSIZE = 16
NEG = -1e30
EXP2_SCALE = math.log2(math.e) / math.sqrt(HD)


B_AXES = ("zl", "y")
NX, NB, NC, NH = 4, 8, 2, 4
ROWS_Q, ROWS_M, ROWS_P, ROWS_O = 128, 96, 16, 32
ROWS_F = 128
NQ = NB * ROWS_Q
HALF = NB * ROWS_M
OFFSETS = (0, 3, 1, 2)


def in_vmem(array):
    return pltpu.with_memory_space_constraint(array, pltpu.VMEM)


VMEM_SPEC = pl.BlockSpec(memory_space=pltpu.VMEM)
SMEM_SPEC = pl.BlockSpec(memory_space=pltpu.SMEM)


def bias_body(place_ref, probe_ref, pattern_ref, bias_ref):
    x = place_ref[0]
    core = place_ref[1]
    pattern = pattern_ref[...].astype(jnp.float32)
    row = lax.broadcasted_iota(jnp.int32, (8, 64), 0)
    own_rows = (x * NB + row) * NC + core
    pick = (lax.broadcasted_iota(jnp.int32, (8, 64), 1) == own_rows).astype(jnp.float32)
    allowed_rows = jnp.dot(pick, pattern, preferred_element_type=jnp.float32)
    per_block = ROWS_M // CSIZE
    per_slot = HALF // CSIZE
    block = lax.broadcasted_iota(jnp.int32, (64, 128), 0)
    col = lax.broadcasted_iota(jnp.int32, (64, 128), 1)
    slot = jnp.where((block % NC) == core, 0, 1)
    first_col = slot * per_slot + ((block // NC) % NB) * per_block
    inside = (col >= first_col) & (col < first_col + per_block)
    allowed = []
    for offset in OFFSETS:
        spread = inside & ((block // (NC * NB)) == lax.rem(x + offset, NX))
        spread = jnp.where(spread, 1.0, 0.0)
        picked = jnp.dot(allowed_rows, spread, preferred_element_type=jnp.float32)
        allowed.append(jnp.where(picked > 0.5, 0.0, NEG))
    lane = lax.broadcasted_iota(jnp.int32, (1, 128), 1)
    targets = []
    for offset in OFFSETS:
        targets.append((lane + lax.rem(x + offset, NX) * 128).astype(jnp.float32))
    for b in range(NB):
        coded = probe_ref[b].astype(jnp.float32)
        source_x = jnp.floor(coded[0:8] * (1.0 / NC))
        code = source_x * 128.0 + coded[8:16]
        code = code + jnp.where(coded[0:8] - NC * source_x == core.astype(jnp.float32), 0.0, float(per_slot))
        code = jnp.concatenate([code] * 16, axis=0).T
        for row in range(0, ROWS_Q, 32):
            live = [jnp.full((32, 128), NEG, jnp.float32)] * NX
            for j in range(8):
                spread = jnp.broadcast_to(code[row : row + 32, j : j + 1], (32, 128))
                for k in range(NX):
                    live[k] = jnp.where(spread == targets[k], allowed[k][b : b + 1, :], live[k])
            for k in range(NX):
                span = slice(b * ROWS_Q + row, b * ROWS_Q + row + 32)
                bias_ref[k, span, :] = live[k].astype(jnp.bfloat16)


def make_bias(place, probe_rows, pattern):
    return pl.pallas_call(
        bias_body,
        in_specs=[SMEM_SPEC, VMEM_SPEC, VMEM_SPEC],
        out_specs=VMEM_SPEC,
        out_shape=pltpu.VMEM((NX, NQ, 128), jnp.bfloat16),
        compiler_params=pltpu.CompilerParams(vmem_limit_bytes=16 << 20),
        name="bias",
    )(place, in_vmem(probe_rows), in_vmem(pattern))


def chunk_body(k, slots, parts, first, last, *refs):
    received_ref, bias_ref = refs[:2]
    count = parts * len(slots)
    kv_refs = refs[2 : 2 + count]
    rest = refs[2 + count :]
    if not first:
        m_in, acc_in = rest[:2]
        rest = rest[2:]
    if last:
        out_ref, score_ref, peak_ref = rest
    else:
        m_out, acc_out, score_ref, peak_ref = rest
    width = 256
    size = HALF * len(slots)
    entry = lax.broadcasted_iota(jnp.int32, (size, 128), 0) // CSIZE + slots[0] * (HALF // CSIZE)
    onehot = (entry == lax.broadcasted_iota(jnp.int32, (size, 128), 1)).astype(jnp.bfloat16)
    if parts == 1:
        keys = [r[:, :ROWS_M, :].reshape(HALF, HD) for r in kv_refs]
        values = [r[:, ROWS_M:, :].reshape(HALF, HD) for r in kv_refs]
    else:
        keys = [r[:, :ROWS_M, :].reshape(HALF, HD) for r in kv_refs[0::2]]
        values = []
        for a_ref, b_ref in zip(kv_refs[0::2], kv_refs[1::2]):
            for n in range(NB):
                values += [a_ref[n, ROWS_M:, :], b_ref[n]]
    keys = jnp.concatenate([jnp.concatenate(keys, axis=0), onehot], axis=1)
    values = jnp.concatenate([jnp.concatenate(values, axis=0), jnp.ones((size, 128), jnp.bfloat16)], axis=1)
    rows = received_ref[:, :ROWS_Q, :].reshape(NQ, HD)
    rows = jnp.concatenate([rows, bias_ref[k]], axis=1)
    for j in range(size // width):
        span = slice(j * width, (j + 1) * width)
        scores = lax.dot_general(rows, keys[span], (((1,), (1,)), ((), ())), preferred_element_type=jnp.float32)
        score_ref[:, span] = scores
        peak = jnp.maximum(scores[:, :128], scores[:, 128:])
        if j:
            peak = jnp.maximum(peak, peak_ref[...])
        peak_ref[...] = peak

    def wide(lanes, times):
        return jnp.concatenate([lanes] * times, axis=1)

    tile = 512 // len(slots) ** 2
    for t in range(NQ // tile):
        span = slice(t * tile, (t + 1) * tile)
        peak = jnp.broadcast_to(jnp.max(peak_ref[span, :], axis=1, keepdims=True), (tile, 128))
        if first:
            peak = jnp.maximum(peak, NEG / 2)
        else:
            old = m_in[span, :]
            peak = jnp.maximum(peak, old)
        weights = jnp.exp2((score_ref[span, :] - wide(peak, size // 128)) * EXP2_SCALE).astype(jnp.bfloat16)
        acc = jnp.dot(weights, values, preferred_element_type=jnp.float32)
        if not first:
            acc = acc + acc_in[span, :] * wide(jnp.exp2((old - peak) * EXP2_SCALE), 2)
        if last:
            out = (acc[:, :HD] / acc[:, HD:]).astype(jnp.bfloat16)
            per = tile // ROWS_Q
            out_ref[t * per : (t + 1) * per] = out.reshape(per, ROWS_Q, HD)
        else:
            m_out[span, :] = peak
            acc_out[span, :] = acc


def attend(k, received, bias, kv, state, slots=(0, 1), last=False):
    first = state is None
    parts = len(kv) // len(slots)
    args = [received, bias, *kv]
    if not first:
        args += list(state)
    if last:
        out_shape = pltpu.VMEM((NB, ROWS_Q, HD), jnp.bfloat16)
    else:
        out_shape = [pltpu.VMEM((NQ, 128), jnp.float32), pltpu.VMEM((NQ, 2 * HD), jnp.float32)]
    return pl.pallas_call(
        lambda *refs: chunk_body(k, slots, parts, first, last, *refs),
        in_specs=[VMEM_SPEC] * len(args),
        out_specs=VMEM_SPEC if last else [VMEM_SPEC] * 2,
        out_shape=out_shape,
        scratch_shapes=[pltpu.VMEM((NQ, HALF * len(slots)), jnp.float32), pltpu.VMEM((NQ, 128), jnp.float32)],
        cost_estimate=pl.CostEstimate(flops=1 << 20, bytes_accessed=1 << 10, transcendentals=0),
        compiler_params=pltpu.CompilerParams(vmem_limit_bytes=24 << 20),
    )(*[in_vmem(arg) for arg in args])


def project_body(order, place_ref, gate_ref, rec_ref, own_ref, w_ref, *outs):
    plane = place_ref[2]
    starts = [pl.multiple_of(lax.rem(plane + away, NH) * ROWS_O, ROWS_O) for away in order]
    mixed = []
    for h in range(NB):
        gate = 1.0 / (1.0 + jnp.exp(jnp.full((1, 128), -gate_ref[h], jnp.float32)))
        span = slice(h * HD, (h + 1) * HD)
        rows = []
        for start in starts:
            recalled = rec_ref[h, pl.ds(start, ROWS_O), :].astype(jnp.float32)
            blended = gate * recalled + (1.0 - gate) * own_ref[pl.ds(start, ROWS_O), span].astype(jnp.float32)
            rows.append(blended.astype(jnp.bfloat16))
        mixed.append(jnp.concatenate(rows, axis=0))
    mixed = jnp.concatenate(mixed, axis=1)
    width = 512
    for i in range(w_ref.shape[1] // width):
        span = slice(i * width, (i + 1) * width)
        part = jnp.dot(mixed, w_ref[:, span], preferred_element_type=jnp.float32)
        row = 0
        for out_ref in outs:
            size = out_ref.shape[0]
            out_ref[:, span] = part[row : row + size].astype(out_ref.dtype)
            row += size


def project(order, place, gate_bias, recalled, own_values, w_out):
    model = w_out.shape[1]
    passed_on = [away for away in order if away]
    outs = [pltpu.VMEM((ROWS_O // 2, model), jnp.bfloat16)] * (2 * len(passed_on))
    if len(passed_on) < len(order):
        outs.append(pltpu.VMEM((ROWS_O, model), jnp.float32))
    return pl.pallas_call(
        lambda *refs: project_body(order, *refs),
        in_specs=[SMEM_SPEC, SMEM_SPEC, VMEM_SPEC, VMEM_SPEC, VMEM_SPEC],
        out_specs=[VMEM_SPEC] * len(outs),
        out_shape=outs,
        cost_estimate=pl.CostEstimate(flops=1 << 20, bytes_accessed=1 << 10, transcendentals=0),
        compiler_params=pltpu.CompilerParams(vmem_limit_bytes=16 << 20),
    )(place, gate_bias, in_vmem(recalled), in_vmem(own_values), in_vmem(w_out))


def add_body(a_ref, b_ref, out_ref):
    out_ref[...] = (a_ref[...].astype(jnp.float32) + b_ref[...].astype(jnp.float32)).astype(jnp.bfloat16)


def add(*args):
    return pl.pallas_call(
        add_body,
        in_specs=[VMEM_SPEC] * 2,
        out_specs=VMEM_SPEC,
        out_shape=pltpu.VMEM(args[0].shape, jnp.bfloat16),
        compiler_params=pltpu.CompilerParams(vmem_limit_bytes=16 << 20),
    )(*[in_vmem(arg) for arg in args])


def finish_body(half, here_ref, a_ref, b_ref, *rest):
    rows = a_ref.shape[0]
    total = here_ref[half * rows : (half + 1) * rows, :] + a_ref[...].astype(jnp.float32) + b_ref[...].astype(jnp.float32)
    rest[-1][...] = total.astype(jnp.bfloat16)


def finish(half, here, a, b, out=None):
    rows, model = a.shape
    block = pl.BlockSpec((rows, model), lambda i: (half, 0))
    args = [in_vmem(here), in_vmem(a), in_vmem(b)]
    in_specs = [VMEM_SPEC] * 3
    if out is not None:
        args.append(out)
        in_specs.append(pl.BlockSpec(memory_space=pl.ANY))
    return pl.pallas_call(
        lambda *refs: finish_body(half, *refs),
        grid=(1,),
        in_specs=in_specs,
        out_specs=block,
        out_shape=jax.ShapeDtypeStruct((2 * rows, model), jnp.bfloat16),
        input_output_aliases={} if out is None else {3: 0},
        compiler_params=pltpu.CompilerParams(vmem_limit_bytes=16 << 20),
    )(*args)


def pack_body(q_ref, k_ref, v_ref, probe_hbm, out_ref, probe_ref, sems):
    probe_copy = pltpu.make_async_copy(probe_hbm, probe_ref, sems.at[3 * NB])
    probe_copy.start()
    copies = []
    for h in range(NB):
        span = slice(h * HD, (h + 1) * HD)
        row = 0
        for source in (q_ref, k_ref, v_ref):
            size = source.shape[0]
            place = out_ref.at[h, row : row + size, :]
            copies.append(pltpu.make_async_copy(source.at[:, span], place, sems.at[len(copies)]))
            row += size
    for copy in copies:
        copy.start()
    probe_copy.wait()
    per_block = ROWS_M // CSIZE
    number = probe_ref[...].astype(jnp.float32)
    block = jnp.floor((number + 0.5) * (1.0 / per_block))
    rest = number - per_block * block
    pair = jnp.floor(block * (1.0 / NC))
    source_x = jnp.floor(block * (1.0 / (NC * NB)))
    column = (pair - NB * source_x) * per_block + rest
    coded = jnp.concatenate([source_x * NC + block - NC * pair, column], axis=0)
    coded = coded.astype(jnp.bfloat16)
    for h in range(NB):
        out_ref[h, ROWS_Q + 2 * ROWS_M :, :] = coded
    for copy in copies:
        copy.wait()


def pack(queries, mem_keys, mem_values, probe_rows):
    anywhere = pl.BlockSpec(memory_space=pltpu.HBM)
    return pl.pallas_call(
        pack_body,
        in_specs=[anywhere] * 4,
        out_specs=VMEM_SPEC,
        out_shape=pltpu.VMEM((NB, ROWS_Q + 2 * ROWS_M + ROWS_P, HD), jnp.bfloat16),
        scratch_shapes=[pltpu.VMEM(probe_rows.shape, probe_rows.dtype), pltpu.SemaphoreType.DMA((3 * NB + 1,))],
        compiler_params=pltpu.CompilerParams(vmem_limit_bytes=16 << 20),
        name="pack",
    )(*[pltpu.with_memory_space_constraint(a, pltpu.HBM) for a in (queries, mem_keys, mem_values, probe_rows)])


def local(queries, mem_keys, mem_values, own_values, gate_bias, w_out, probes, pattern):
    received = lax.all_to_all(pack(queries, mem_keys, mem_values, probes.T), B_AXES, 0, 0, tiled=True)
    own = received[:, ROWS_Q : ROWS_Q + 2 * ROWS_M, :]

    def shift(array, by):
        return lax.ppermute(array, "x", [(i, (i + by) % NX) for i in range(NX)])

    def swap(array):
        return lax.ppermute(array, "c", [(0, 1), (1, 0)])

    place = jnp.stack([lax.axis_index("x"), lax.axis_index("c"), lax.axis_index("h")]).astype(jnp.int32)
    left = shift(own, 1)
    right = shift(own, 3)
    own_far = swap(own)
    bias = make_bias(place, received[:, ROWS_Q + 2 * ROWS_M :, :], pattern)
    state = attend(0, received, bias, (own, own_far), None)
    left, *state = lax.optimization_barrier((left, *state))
    opposite_k = shift(left[:, :ROWS_F], 1)
    left_far = swap(left)
    right, *state = lax.optimization_barrier((right, *state))
    opposite_v = shift(right[:, ROWS_F:], 3)
    right_far = swap(right)
    state = attend(1, received, bias, (left, left_far), state)
    state = attend(2, received, bias, (right, right_far), state)
    opposite_k, opposite_v, *state = lax.optimization_barrier((opposite_k, opposite_v, *state))
    opposite_far = (swap(opposite_k), swap(opposite_v))
    state = attend(3, received, bias, (opposite_k, opposite_v), state, slots=(0,))
    state = attend(3, received, bias, opposite_far, state, slots=(1,), last=True)
    recalled = lax.all_to_all(state, B_AXES, 0, 0, tiled=True)

    def plane_shift(array, by):
        return lax.ppermute(array, "h", [(i, (i + by) % NH) for i in range(NH)])

    operands = (place, gate_bias, recalled, own_values, w_out)
    top, bottom = project((2,), *operands)
    top = plane_shift(top, 1)
    bottom = plane_shift(bottom, 3)
    up, up_free, down_free, down, here = project((1, 3, 0), *operands)
    up_free = plane_shift(up_free, 1)
    down_free = plane_shift(down_free, 3)
    up = plane_shift(add(up, top), 1)
    down = plane_shift(add(down, bottom), 3)
    out = finish(1, here, up_free, down)
    return finish(0, here, up, down_free, out)


def solution(mesh):
    fine = Mesh(mesh.devices.reshape(NX, 2, 4, NC, 4), ("x", "zl", "y", "c", "h"))
    mem = ("x", "zl", "y", "c")
    in_specs = (
        P(mem, "h"),
        P(mem, "h"),
        P(mem, "h"),
        P(mem, "h"),
        P("h"),
        P("h", None),
        P(mem, None),
        P(),
    )

    return jax.shard_map(local, mesh=fine, in_specs=in_specs, out_specs=P((*mem, "h"), None), check_vma=False)
```
